256 devices in a mesh: dp: 32 (over y_lo, z, core), tensor: 8 (over y_hi, x).
Axes of the slice: x: 4, y: 4 (y_hi: 2, y_lo: 2; y = y_hi * 2 + y_lo), z: 8, core: 2. Of those that a mesh axis runs over, the one named last changes fastest.
Arguments:
- activations: bfloat16 [1024, 16384], P('dp', 'tensor'), may hold values from -6 to 6
- weight: bfloat16 [16384, 16384], P('tensor', 'dp'), may hold values from -0.046875 to 0.046875
- out_grad: bfloat16 [1024, 16384], P('tensor', 'dp'), may hold values from -6 to 6
Outputs:
- outputs: bfloat16 [1024, 16384], P('tensor', 'dp')
- in_grad: bfloat16 [1024, 16384], P('dp', 'tensor')
- weight_grad: float32 [16384, 16384], P('tensor', 'dp')
The draws below stay inside these ranges and needn't reach their ends.
All inputs are finite; a program needn't handle non-finite values.
Results may differ from the reference program's by a relative error of at most 0.0049.
Values may be sent and summed in bfloat16 or wider, within the bound.
A program may use at most 64 MiB of HBM per device.

```python
import math
import jax
import jax.numpy as jnp
from jax import lax

D = 16384
F = 16384
TOKENS = 1024


def level_of(rng, dims, split, low, largest):
    def one(dim, parts):
        steps = jax.random.uniform(jax.random.fold_in(jax.random.fold_in(rng, 6), dim), (parts,), jnp.float32, low / len(split), largest / len(split))
        return jnp.repeat(jnp.exp(steps), dims[dim] // parts).reshape((-1,) + (1,) * (len(dims) - dim - 1))

    factor_of = one(*split[0])
    for cut in split[1:]:
        factor_of = factor_of * one(*cut)
    return factor_of


def noise(key, extent, scale, most, cuts=(), held_as=jnp.bfloat16):
    drawn = jax.random.normal(key, extent, jnp.float32) * scale
    if len(cuts) > 0:
        drawn = level_of(key, extent, cuts, -0.22, 0.18) * drawn
    return jnp.clip(drawn, min=-most, max=most).astype(held_as)


def setup_inputs(seed: int = 0) -> dict:
    seeds = jax.random.split(jax.random.key(seed), 4)
    return {
        "activations": noise(seeds[0], (TOKENS, D), 1.0, 6.0, ((0, 32), (1, 8))),
        "weight": noise(seeds[1], (D, F), D ** -0.5, 0.046875, ((0, 8), (1, 32))),
        "out_grad": noise(seeds[2], (TOKENS, F), 1.0, 6.0, ((0, 8), (1, 32))),
    }


def signs_table(width):
    position = jnp.arange(width, dtype=jnp.int32)
    joined = jnp.bitwise_and(position[:, None], position[None, :])
    parity = jnp.zeros_like(joined)
    for bit_number in range(width.bit_length() - 1):
        parity = parity + jnp.bitwise_and(jnp.right_shift(joined, bit_number), 1)
    return jnp.where(parity % 2 == 1, -1.0, 1.0).astype(jnp.float32)

def transform(values, width):
    bit_count = width.bit_length() - 1
    first_size = 2 ** (bit_count // 2)
    second = width // first_size
    shaped = values.reshape(values.shape[0], first_size, second)
    result = jnp.einsum('rab,ac->rcb', shaped, signs_table(first_size), precision=lax.Precision.HIGHEST)
    result = jnp.einsum('rcb,bd->rcd', result, signs_table(second), precision=lax.Precision.HIGHEST)
    return result.reshape(values.shape[0], width)

def reference(activations, weight, out_grad):
    factor = 1.0 / math.sqrt(D)
    rotated = (transform(activations.astype(jnp.float32), D) * factor).astype(jnp.bfloat16)
    outputs = jnp.dot(rotated, weight, preferred_element_type=jnp.float32).astype(jnp.bfloat16)
    weight_grad = lax.dot_general(rotated, out_grad, (((0,), (0,)), ((), ())), preferred_element_type=jnp.float32) * (1.0 / math.sqrt(TOKENS))
    rotated_grad = lax.dot_general(out_grad, weight, (((1,), (1,)), ((), ())), preferred_element_type=jnp.float32)
    in_grad = (transform(rotated_grad, D) * factor).astype(jnp.bfloat16)
    return (outputs, in_grad, weight_grad)
```

```python
import functools
import math

import jax
import jax.numpy as jnp
import numpy as np
from jax import lax
from jax.experimental import pallas as pl
from jax.experimental.pallas import tpu as pltpu
from jax.sharding import PartitionSpec as P

MESH = pl.DeviceIdType.MESH
YL, Z, C, T = 2, 8, 2, 8
F32, BF16 = jnp.float32, jnp.bfloat16
SEMS = 256


def signs_table(width):
    position = np.arange(width)
    joined = position[:, None] & position[None, :]
    parity = np.zeros_like(joined)
    for bit_number in range(width.bit_length() - 1):
        parity = parity + ((joined >> bit_number) & 1)
    return np.where(parity % 2 == 1, -1.0, 1.0)


def butterfly(parts):
    parts = list(parts)
    apart = 1
    while apart < len(parts):
        for low in range(len(parts)):
            if low & apart == 0:
                a, b = parts[low], parts[low | apart]
                parts[low], parts[low | apart] = a + b, a - b
        apart *= 2
    return parts


def kernel(scale, grad_scale, act, w, og, had, out, ing, wg, w2, s1, x1, s2, r, g, g2, pf,
           sbp, sbm, rp, rm, ys, yr, q, xq, t1, v1, t2, igb, wgv, rg, sems, local_sems):
    d, t = lax.axis_index("dp"), lax.axis_index("tensor")
    c, z, yl = d % C, (d // C) % Z, d // (C * Z)
    tokens, width = act.shape
    chunk = width // T

    def block(rel, zz, core):
        return (((yl + rel) % YL) * Z + (zz + 2 * Z) % Z) * C + core

    sib = (block(0, z, 1 - c), t)
    zp, zm = (block(0, z + 1, c), t), (block(0, z - 1, c), t)
    yp = (block(1, z, c), t)
    peers = [(d, (t + j) % T) for j in range(1, T)]

    barrier = pltpu.get_barrier_semaphore()
    everyone = [sib, zp, zm, yp] + peers
    for other in everyone:
        pl.semaphore_signal(barrier, inc=1, device_id=other, device_id_type=MESH)
    pl.semaphore_wait(barrier, len(everyone))

    used = [0]
    sent = []

    def pair():
        used[0] += 2
        return used[0] - 2

    def remote(src, dst, to, number):
        return pltpu.make_async_remote_copy(
            src_ref=src, dst_ref=dst, send_sem=sems.at[number], recv_sem=sems.at[number + 1],
            device_id=to, device_id_type=MESH)

    def send(src, dst, to, number):
        copy = remote(src, dst, to, number)
        copy.start()
        sent.append(copy)

    def arrive(dst, number):
        remote(dst, dst, sib, number).wait_recv()

    def local_rotation(parts):
        rows = jnp.concatenate(parts, axis=0)
        table = had[...]
        if rows.dtype == BF16:
            mixed = jnp.dot(rows, table, preferred_element_type=F32)
        else:
            high = rows.astype(BF16)
            rest = rows - high.astype(F32)
            middle = rest.astype(BF16)
            low = (rest - middle.astype(F32)).astype(BF16)
            mixed = (jnp.dot(high, table, preferred_element_type=F32)
                     + jnp.dot(middle, table, preferred_element_type=F32)
                     + jnp.dot(low, table, preferred_element_type=F32))
        return butterfly([mixed[k * tokens:(k + 1) * tokens] for k in range(T)])

    def rotate(parts, first, first_in, second, landing):
        for k, part in enumerate(local_rotation(parts)):
            first[k] = part
        numbers = [pair() for _ in peers]
        for j, peer in enumerate(peers):
            send(first.at[peer[1]], first_in.at[t], peer, numbers[j])
        first_in[t] = first[t]
        for j in range(1, T):
            arrive(first_in.at[(t + T - j) % T], numbers[j - 1])
        for k, part in enumerate(butterfly([first_in[k] for k in range(T)])):
            second[k] = (part * scale).astype(BF16)
        numbers = [pair() for _ in peers]
        for j, peer in enumerate(peers):
            send(second.at[peer[1]], landing.at[t], peer, numbers[j])
        landing[t] = second[t]

        def finish():
            for j in range(1, T):
                arrive(landing.at[(t + T - j) % T], numbers[j - 1])

        return finish

    w_number = pair()
    send(w, w2, sib, w_number)

    own = block(0, z, c)
    finish = rotate([act[:, k * chunk:(k + 1) * chunk] for k in range(T)], s1, x1, s2, r.at[own])

    gather_numbers = [pair() for _ in peers]
    for j, peer in enumerate(peers):
        send(og, g.at[pl.ds(2 * t, 2)], peer, gather_numbers[j])
    g[pl.ds(2 * t, 2)] = og[...]

    finish()

    to_sib = []

    def share(rel, zz):
        number = pair()
        send(r.at[block(rel, zz, c)], r.at[block(rel, zz, c)], sib, number)
        to_sib.append((block(rel, zz, 1 - c), number))

    numbers = {(sign, rel, s): pair() for sign in (1, -1) for rel in (0, 1) for s in range(4)}

    def pass_on(sign, rel, zz, s):
        b = block(rel, zz, c)
        send(r.at[b], r.at[b], zp if sign == 1 else zm, numbers[sign, rel, s])

    y_number = pair()
    send(r.at[own], r.at[own], yp, y_number)
    pass_on(1, 0, z, 0)
    pass_on(-1, 0, z, 0)
    share(0, z)
    arrive(r.at[block(1, z, c)], y_number)
    pass_on(1, 1, z, 0)
    pass_on(-1, 1, z, 0)
    share(1, z)

    def ring_step(s):
        for rel in (0, 1):
            for sign in (1, -1):
                keep = 0 if sign == 1 else 1
                if s == 3 and rel != keep:
                    continue
                zz = z - sign * (1 + s)
                arrive(r.at[block(rel, zz, c)], numbers[sign, rel, s])
                if s < 2 or (s == 2 and rel == keep):
                    pass_on(sign, rel, zz, s + 1)
                share(rel, zz)

    ring_step(0)
    for j in range(1, T):
        arrive(g.at[pl.ds(2 * ((t + T - j) % T), 2)], gather_numbers[j - 1])
    g2_number = pair()
    send(g.at[:, 1 - c], g2, sib, g2_number)
    ring_step(1)
    arrive(g2, g2_number)
    arrive(w2, w_number)

    rows = Z * YL * tokens

    def partial(k, carry):
        mine = g[:, c].reshape(rows, g.shape[-1])
        theirs = g2[...].reshape(rows, g.shape[-1])
        at = pl.ds(pl.multiple_of(k * chunk, chunk), chunk)
        dims = (((1,), (1,)), ((), ()))
        total = (lax.dot_general(mine, w[at, :], dims, preferred_element_type=F32)
                 + lax.dot_general(theirs, w2[at, :], dims, preferred_element_type=F32))
        pf[:, k] = total.reshape(Z * YL, tokens, chunk)
        return carry

    lax.fori_loop(0, T, partial, 0)
    ring_step(2)

    sums = {(sign, rel, s): pair() for sign in (1, -1) for rel in (0, 1) for s in range(4)}

    def reduce_step(s):
        for rel in (0, 1):
            for sign in (1, -1):
                keep = 0 if sign == 1 else 1
                if s == 0 and rel != keep:
                    continue
                into, out_of, to = (rp, sbp, zp) if sign == 1 else (rm, sbm, zm)
                target = block(rel, z + sign * (4 - s), 0) // C
                total = pf[target]
                if s > 1 or (s == 1 and rel == keep):
                    arrive(into.at[rel, s - 1], sums[sign, rel, s - 1])
                    total = total + into[rel, s - 1].astype(F32)
                out_of[rel, s] = total.astype(BF16)
                send(out_of.at[rel, s], into.at[rel, s], to, sums[sign, rel, s])

    reduce_step(0)
    ring_step(3)
    for b, number in to_sib:
        arrive(r.at[b], number)

    def products(i, carry):
        total = jnp.zeros((256, w.shape[1]), F32)
        for k in range(T):
            lhs = r[pl.ds(8 * i, 8), k].reshape(256, chunk)
            total = total + jnp.dot(lhs, w[k * chunk:(k + 1) * chunk, :], preferred_element_type=F32)
        q[pl.ds(2 * i, 2)] = total.reshape(2, 128, w.shape[1]).astype(BF16)
        return carry

    lax.fori_loop(0, 4, products, 0)
    out_numbers = [pair() for _ in peers]
    for j, peer in enumerate(peers):
        send(q.at[peer[1]], xq.at[t], peer, out_numbers[j])
    xq[t] = q[t]

    def weight_grad(k, carry):
        lhs = r[:, k].reshape(2 * rows, chunk)
        rhs = g[...].reshape(2 * rows, g.shape[-1])
        total = lax.dot_general(lhs, rhs, (((0,), (0,)), ((), ())), preferred_element_type=F32)
        at = pl.ds(pl.multiple_of(k * chunk, chunk), chunk)
        wgv[at, :] = total * grad_scale
        pltpu.make_async_copy(wgv.at[at, :], wg.at[at, :], local_sems.at[k]).start()
        return carry

    reduce_step(1)
    lax.fori_loop(0, 3, weight_grad, 0)
    reduce_step(2)
    lax.fori_loop(3, 6, weight_grad, 0)
    reduce_step(3)
    lax.fori_loop(6, 8, weight_grad, 0)

    finals = []
    for rel in (1, 0):
        total = pf[block(rel, z, 0) // C]
        for sign, into in ((1, rp), (-1, rm)):
            arrive(into.at[rel, 3], sums[sign, rel, 3])
            total = total + into[rel, 3].astype(F32)
        if rel == 1:
            ys[...] = total.astype(BF16)
            back_number = pair()
            send(ys, yr, yp, back_number)
        else:
            rg[...] = total
    arrive(yr, back_number)
    finish = rotate([rg[k] + yr[k].astype(F32) for k in range(T)], t1, v1, t2, igb)

    for j in range(1, T):
        arrive(xq.at[(t + T - j) % T], out_numbers[j - 1])
    total = xq[0].astype(F32)
    for k in range(1, T):
        total = total + xq[k].astype(F32)
    out[...] = total.astype(BF16)

    finish()
    for k in range(T):
        ing[:, k * chunk:(k + 1) * chunk] = igb[k]

    for copy in sent:
        copy.wait_send()

    def written(k, carry):
        at = pl.ds(pl.multiple_of(k * chunk, chunk), chunk)
        pltpu.make_async_copy(wgv.at[at, :], wg.at[at, :], local_sems.at[k]).wait()
        return carry

    lax.fori_loop(0, 8, written, 0)
    assert used[0] <= SEMS, used[0]


def per_device(activations, weight, out_grad):
    tokens, width = activations.shape
    features = weight.shape[1]
    groups = YL * Z * C
    chunk = width // T
    scale = 1.0 / math.sqrt(width * T)
    grad_scale = 1.0 / math.sqrt(tokens * groups)
    had = jnp.asarray(signs_table(chunk), BF16)
    vmem = pl.BlockSpec(memory_space=pltpu.VMEM)
    part = (T, tokens, chunk)
    return pl.pallas_call(
        functools.partial(kernel, scale, grad_scale),
        out_shape=(
            jax.ShapeDtypeStruct((out_grad.shape[0], features), BF16),
            jax.ShapeDtypeStruct((tokens, width), BF16),
            jax.ShapeDtypeStruct((width, features), F32),
        ),
        in_specs=[vmem] * 4,
        out_specs=(vmem, vmem, pl.BlockSpec(memory_space=pl.ANY)),
        scratch_shapes=[
            pltpu.VMEM((width, features), BF16),
            pltpu.VMEM(part, F32), pltpu.VMEM(part, F32), pltpu.VMEM(part, BF16),
            pltpu.VMEM((groups,) + part, BF16),
            pltpu.VMEM((groups // C, C, tokens, features), BF16),
            pltpu.VMEM((groups // C, tokens, features), BF16),
            pltpu.VMEM((groups // C,) + part, F32),
            pltpu.VMEM((2, 4) + part, BF16), pltpu.VMEM((2, 4) + part, BF16),
            pltpu.VMEM((2, 4) + part, BF16), pltpu.VMEM((2, 4) + part, BF16),
            pltpu.VMEM(part, BF16), pltpu.VMEM(part, BF16),
            pltpu.VMEM((T, out_grad.shape[0], features), BF16),
            pltpu.VMEM((T, out_grad.shape[0], features), BF16),
            pltpu.VMEM(part, F32), pltpu.VMEM(part, F32),
            pltpu.VMEM(part, BF16), pltpu.VMEM(part, BF16),
            pltpu.VMEM((width, features), F32),
            pltpu.VMEM(part, F32),
            pltpu.SemaphoreType.DMA((SEMS,)),
            pltpu.SemaphoreType.DMA((T,)),
        ],
        compiler_params=pltpu.CompilerParams(
            collective_id=0, has_side_effects=True, vmem_limit_bytes=56 << 20),
        name="rotated_projection",
    )(activations, weight, out_grad.reshape(2, C, tokens, features), had)


def solution(mesh):
    return jax.shard_map(
        per_device,
        mesh=mesh,
        in_specs=(P("dp", "tensor"), P("tensor", "dp"), P("tensor", "dp")),
        out_specs=(P("tensor", "dp"), P("dp", "tensor"), P("tensor", "dp")),
        check_vma=False,
    )
```

```python
import functools
import math

import jax
import jax.numpy as jnp
import numpy as np
from jax import lax
from jax.experimental import pallas as pl
from jax.experimental.pallas import tpu as pltpu
from jax.sharding import PartitionSpec as P

MESH = pl.DeviceIdType.MESH
YL, Z, C, T, X = 2, 8, 2, 8, 4
LO_CHUNKS = 4
F32, BF16 = jnp.float32, jnp.bfloat16
SEMS = 320


def signs_table(width):
    position = np.arange(width)
    joined = position[:, None] & position[None, :]
    parity = np.zeros_like(joined)
    for bit_number in range(width.bit_length() - 1):
        parity = parity + ((joined >> bit_number) & 1)
    return np.where(parity % 2 == 1, -1.0, 1.0)


def butterfly(parts):
    parts = list(parts)
    apart = 1
    while apart < len(parts):
        for low in range(len(parts)):
            if low & apart == 0:
                a, b = parts[low], parts[low | apart]
                parts[low], parts[low | apart] = a + b, a - b
        apart *= 2
    return parts


def kernel(scale, grad_scale, lo_chunks, act_hbm, w_hbm, og_hbm, had_hbm, out, ing, wg, act, w, og, had,
           w2, s1, x1, s2, r, g, g2, pf, sbp, sbm, rp, rm, ybs, ybr, ys, yr, q, xq, t1, v1, t2, igb,
           wgv, rg, sems, local_sems):
    d, t = lax.axis_index("dp"), lax.axis_index("tensor")
    c, z, yl = d % C, (d // C) % Z, d // (C * Z)
    yh, x = t // X, t % X
    ahead = 1 - 2 * c
    tokens, width = act.shape
    chunk = width // T
    lo, hi = pl.ds(0, lo_chunks), pl.ds(lo_chunks, T - lo_chunks)

    def block(rel, zz, core):
        return (((yl + rel) % YL) * Z + (zz + 2 * Z) % Z) * C + core

    sib = (block(0, z, 1 - c), t)
    zp, zm = (block(0, z + ahead, c), t), (block(0, z - ahead, c), t)
    yp = (block(1, z, c), t)
    peers = [(d, (t + j) % T) for j in range(1, T)]
    opposite = (d, (t + X) % T)
    along_x = [(d, yh * X + (x + j) % X) for j in range(1, X)]

    barrier = pltpu.get_barrier_semaphore()
    everyone = [sib, zp, zm, yp] + peers
    for other in everyone:
        pl.semaphore_signal(barrier, inc=1, device_id=other, device_id_type=MESH)
    loads = [pltpu.make_async_copy(src, dst, local_sems.at[T + i])
             for i, (src, dst) in enumerate(((act_hbm, act), (had_hbm, had), (og_hbm, og), (w_hbm, w)))]
    for load in loads:
        load.start()
    loads[0].wait()
    loads[1].wait()

    used = [0]
    sent = []

    def pair():
        used[0] += 2
        return used[0] - 2

    def remote(src, dst, to, number):
        return pltpu.make_async_remote_copy(
            src_ref=src, dst_ref=dst, send_sem=sems.at[number], recv_sem=sems.at[number + 1],
            device_id=to, device_id_type=MESH)

    def send(src, dst, to, number):
        copy = remote(src, dst, to, number)
        copy.start()
        sent.append(copy)

    def arrive(dst, number):
        remote(dst, dst, sib, number).wait_recv()

    def local_rotation(parts):
        rows = jnp.concatenate(parts, axis=0)
        table = had[...]
        if rows.dtype == BF16:
            mixed = jnp.dot(rows, table, preferred_element_type=F32)
        else:
            high = rows.astype(BF16)
            rest = rows - high.astype(F32)
            middle = rest.astype(BF16)
            low = (rest - middle.astype(F32)).astype(BF16)
            mixed = (jnp.dot(high, table, preferred_element_type=F32)
                     + jnp.dot(middle, table, preferred_element_type=F32)
                     + jnp.dot(low, table, preferred_element_type=F32))
        return butterfly([mixed[k * tokens:(k + 1) * tokens] for k in range(T)])

    def rotate_first(first, first_in):
        numbers = [pair() for _ in peers]
        for j, peer in enumerate(peers):
            send(first.at[peer[1]], first_in.at[t], peer, numbers[j])
        first_in[t] = first[t]
        for j in range(1, T):
            arrive(first_in.at[(t + T - j) % T], numbers[j - 1])

    def rotate_second(first_in, second, landing):
        for k, part in enumerate(butterfly([first_in[k] for k in range(T)])):
            second[k] = (part * scale).astype(BF16)
        numbers = [pair() for _ in peers]
        for j, peer in enumerate(peers):
            send(second.at[peer[1]], landing.at[t], peer, numbers[j])
        landing[t] = second[t]

        def finish():
            for j in range(1, T):
                arrive(landing.at[(t + T - j) % T], numbers[j - 1])

        return finish

    own = block(0, z, c)
    for k, part in enumerate(local_rotation([act[:, k * chunk:(k + 1) * chunk] for k in range(T)])):
        s1[k] = part
    pl.semaphore_wait(barrier, len(everyone))
    rotate_first(s1, x1)
    loads[2].wait()

    def grad_rows(tt):
        return g.at[pl.ds(2 * tt, 2)]

    opposite_number = pair()
    send(og, grad_rows(t), opposite, opposite_number)
    finish = rotate_second(x1, s2, r.at[own])
    near_numbers = [pair() for _ in along_x]
    for j, peer in enumerate(along_x):
        send(og, grad_rows(t), peer, near_numbers[j])
    g[pl.ds(2 * t, 2)] = og[...]
    loads[3].wait()
    w_number = pair()
    send(w, w2, sib, w_number)
    finish()

    to_sib = []

    def share(rel, zz, part):
        number = pair()
        send(r.at[block(rel, zz, c), part], r.at[block(rel, zz, c), part], sib, number)
        to_sib.append((block(rel, zz, 1 - c), part, number))

    numbers = {(sign, rel, s): pair() for sign in (1, -1) for rel in (0, 1) for s in range(4)}
    whole = pl.ds(0, T)
    parts = (whole, lo)
    across_numbers = {}

    def pass_on(sign, rel, zz, s):
        view = r.at[block(rel, zz, c), parts[rel]]
        send(view, view, zp if sign == 1 else zm, numbers[sign, rel, s])

    def across(zz, step):
        across_numbers[step] = pair()
        view = r.at[block(0, zz, c), hi]
        send(view, view, yp, across_numbers[step])

    def across_arrive(zz, step):
        arrive(r.at[block(1, zz, c), hi], across_numbers[step])
        share(1, zz, hi)

    y_number = pair()
    send(r.at[own, lo], r.at[own, lo], yp, y_number)
    pass_on(1, 0, z, 0)
    pass_on(-1, 0, z, 0)
    across(z, 0)
    share(0, z, whole)
    opposite_t = (t + X) % T
    arrive(grad_rows(opposite_t), opposite_number)
    far_numbers = [pair() for _ in along_x]
    for j, peer in enumerate(along_x):
        send(grad_rows(opposite_t), grad_rows(opposite_t), peer, far_numbers[j])
    arrive(r.at[block(1, z, c), lo], y_number)
    pass_on(1, 1, z, 0)
    pass_on(-1, 1, z, 0)
    share(1, z, lo)

    def ring_step(s):
        for rel in (0, 1):
            for sign in (1, -1):
                keep = 0 if sign == 1 else 1
                if s == 3 and rel != keep:
                    continue
                zz = z - sign * ahead * (1 + s)
                arrive(r.at[block(rel, zz, c), parts[rel]], numbers[sign, rel, s])
                if s < 2 or (s == 2 and rel == keep):
                    pass_on(sign, rel, zz, s + 1)
                if rel == 0:
                    across(zz, sign * (1 + s))
                share(rel, zz, parts[rel])

    def across_step(s):
        for sign in (1, -1):
            if s < 3 or sign == 1:
                across_arrive(z - sign * ahead * (1 + s), sign * (1 + s))

    ring_step(0)
    for j in range(1, X):
        from_x = (x + X - j) % X
        arrive(grad_rows(yh * X + from_x), near_numbers[j - 1])
        arrive(grad_rows((1 - yh) * X + from_x), far_numbers[j - 1])
    g2_number = pair()
    send(g.at[:, 1 - c], g2, sib, g2_number)
    across_arrive(z, 0)
    ring_step(1)
    arrive(g2, g2_number)
    arrive(w2, w_number)

    rows = Z * YL * tokens

    def partial(k, carry):
        mine = g[:, c].reshape(rows, g.shape[-1])
        theirs = g2[...].reshape(rows, g.shape[-1])
        at = pl.ds(pl.multiple_of(k * chunk, chunk), chunk)
        dims = (((1,), (1,)), ((), ()))
        total = (lax.dot_general(mine, w[at, :], dims, preferred_element_type=F32)
                 + lax.dot_general(theirs, w2[at, :], dims, preferred_element_type=F32))
        pf[:, k] = total.reshape(Z * YL, tokens, chunk)
        return carry

    lax.fori_loop(0, T, partial, 0)

    sums = {(sign, rel, s): pair() for sign in (1, -1) for rel in (0, 1) for s in range(4)}
    back_numbers = {}

    def target(rel, zz):
        return block(rel, zz, 0) // C

    def give_across(away):
        i = away + 4
        ybs[i] = pf[target(1, z + ahead * away), hi].astype(BF16)
        back_numbers[away] = pair()
        send(ybs.at[i], ybr.at[i], yp, back_numbers[away])

    def reduce_step(s):
        for rel in (0, 1):
            for sign in (1, -1):
                keep = 0 if sign == 1 else 1
                if s == 0 and rel != keep:
                    continue
                into, out_of, to = (rp, sbp, zp) if sign == 1 else (rm, sbm, zm)
                away = sign * (4 - s)
                at = target(rel, z + ahead * away)
                more = s > 1 or (s == 1 and rel == keep)
                if more:
                    arrive(into.at[rel, s - 1, parts[rel]], sums[sign, rel, s - 1])
                total = pf[at, lo]
                if more:
                    total = total + into[rel, s - 1, lo].astype(F32)
                out_of[rel, s, lo] = total.astype(BF16)
                if rel == 0:
                    arrive(ybr.at[away + 4], back_numbers[away])
                    total = pf[at, hi] + ybr[away + 4].astype(F32)
                    if more:
                        total = total + into[rel, s - 1, hi].astype(F32)
                    out_of[rel, s, hi] = total.astype(BF16)
                send(out_of.at[rel, s, parts[rel]], into.at[rel, s, parts[rel]], to, sums[sign, rel, s])

    for away in (4, 3, -3, 2, -2, 1, -1, 0):
        give_across(away)
    reduce_step(0)
    ring_step(2)
    across_step(0)
    reduce_step(1)
    ring_step(3)
    across_step(1)
    across_step(2)

    def products(i, carry):
        total = jnp.zeros((256, w.shape[1]), F32)
        for k in range(T):
            lhs = r[pl.ds(8 * i, 8), k].reshape(256, chunk)
            total = total + jnp.dot(lhs, w[k * chunk:(k + 1) * chunk, :], preferred_element_type=F32)
        q[pl.ds(2 * i, 2)] = total.reshape(2, 128, w.shape[1]).astype(BF16)
        return carry

    def weight_grad(k, carry):
        lhs = r[:, k].reshape(2 * rows, chunk)
        rhs = g[...].reshape(2 * rows, g.shape[-1])
        total = lax.dot_general(lhs, rhs, (((0,), (0,)), ((), ())), preferred_element_type=F32)
        at = pl.ds(pl.multiple_of(k * chunk, chunk), chunk)
        wgv[at, :] = total * grad_scale
        pltpu.make_async_copy(wgv.at[at, :], wg.at[at, :], local_sems.at[k]).start()
        return carry

    across_step(3)
    for b, part, number in to_sib:
        arrive(r.at[b, part], number)
    lax.fori_loop(0, 4, products, 0)
    out_numbers = [pair() for _ in peers]
    for j, peer in enumerate(peers):
        send(q.at[peer[1]], xq.at[t], peer, out_numbers[j])
    xq[t] = q[t]

    reduce_step(2)
    lax.fori_loop(0, 4, weight_grad, 0)
    reduce_step(3)
    lax.fori_loop(4, 8, weight_grad, 0)

    total = pf[target(1, z), lo]
    for sign, into in ((1, rp), (-1, rm)):
        arrive(into.at[1, 3, lo], sums[sign, 1, 3])
        total = total + into[1, 3, lo].astype(F32)
    ys[...] = total.astype(BF16)
    back_number = pair()
    send(ys, yr, yp, back_number)
    total = pf[target(0, z)]
    for sign, into in ((1, rp), (-1, rm)):
        arrive(into.at[0, 3], sums[sign, 0, 3])
        total = total + into[0, 3].astype(F32)
    rg[...] = total
    arrive(ybr.at[4], back_numbers[0])
    rg[hi] = rg[hi] + ybr[4].astype(F32)
    arrive(yr, back_number)
    rg[lo] = rg[lo] + yr[...].astype(F32)
    for k, part in enumerate(local_rotation([rg[k] for k in range(T)])):
        t1[k] = part
    rotate_first(t1, v1)
    finish = rotate_second(v1, t2, igb)

    for j in range(1, T):
        arrive(xq.at[(t + T - j) % T], out_numbers[j - 1])
    total = xq[0].astype(F32)
    for k in range(1, T):
        total = total + xq[k].astype(F32)
    out[...] = total.astype(BF16)

    finish()
    for k in range(T):
        ing[:, k * chunk:(k + 1) * chunk] = igb[k]

    for copy in sent:
        copy.wait_send()

    def written(k, carry):
        at = pl.ds(pl.multiple_of(k * chunk, chunk), chunk)
        pltpu.make_async_copy(wgv.at[at, :], wg.at[at, :], local_sems.at[k]).wait()
        return carry

    lax.fori_loop(0, 8, written, 0)
    assert used[0] <= SEMS, used[0]


def place(pieces, *refs):
    sems = refs[-1]
    half = (len(refs) - 1) // 2
    copies = []
    for src, dst, count in zip(refs[:half], refs[half:2 * half], pieces):
        step = src.shape[0] // count
        for i in range(count):
            at = pl.ds(i * step, step)
            copies.append(pltpu.make_async_copy(src.at[at], dst.at[at], sems.at[len(copies)]))
    for copy in copies:
        copy.start()
    for copy in copies:
        copy.wait()


def per_device(activations, weight, out_grad):
    tokens, width = activations.shape
    features = weight.shape[1]
    groups = YL * Z * C
    chunk = width // T
    scale = 1.0 / math.sqrt(width * T)
    grad_scale = 1.0 / math.sqrt(tokens * groups)
    had = jnp.asarray(signs_table(chunk), BF16)
    vmem = pl.BlockSpec(memory_space=pltpu.VMEM)
    anywhere = pl.BlockSpec(memory_space=pl.ANY)
    part = (T, tokens, chunk)
    low = (LO_CHUNKS, tokens, chunk)
    high = (T - LO_CHUNKS, tokens, chunk)
    shapes = (
        jax.ShapeDtypeStruct((out_grad.shape[0], features), BF16),
        jax.ShapeDtypeStruct((tokens, width), BF16),
        jax.ShapeDtypeStruct((width, features), F32),
    )
    results = pl.pallas_call(
        functools.partial(kernel, scale, grad_scale, LO_CHUNKS),
        out_shape=shapes,
        in_specs=[anywhere] * 4,
        out_specs=(vmem, vmem, anywhere),
        scratch_shapes=[
            pltpu.VMEM((tokens, width), BF16),
            pltpu.VMEM((width, features), BF16),
            pltpu.VMEM((2, C, tokens, features), BF16),
            pltpu.VMEM((chunk, chunk), BF16),
            pltpu.VMEM((width, features), BF16),
            pltpu.VMEM(part, F32), pltpu.VMEM(part, F32), pltpu.VMEM(part, BF16),
            pltpu.VMEM((groups,) + part, BF16),
            pltpu.VMEM((groups // C, C, tokens, features), BF16),
            pltpu.VMEM((groups // C, tokens, features), BF16),
            pltpu.VMEM((groups // C,) + part, F32),
            pltpu.VMEM((2, 4) + part, BF16), pltpu.VMEM((2, 4) + part, BF16),
            pltpu.VMEM((2, 4) + part, BF16), pltpu.VMEM((2, 4) + part, BF16),
            pltpu.VMEM((9,) + high, BF16), pltpu.VMEM((9,) + high, BF16),
            pltpu.VMEM(low, BF16), pltpu.VMEM(low, BF16),
            pltpu.VMEM((T, out_grad.shape[0], features), BF16),
            pltpu.VMEM((T, out_grad.shape[0], features), BF16),
            pltpu.VMEM(part, F32), pltpu.VMEM(part, F32),
            pltpu.VMEM(part, BF16), pltpu.VMEM(part, BF16),
            pltpu.VMEM((width, features), F32),
            pltpu.VMEM(part, F32),
            pltpu.SemaphoreType.DMA((SEMS,)),
            pltpu.SemaphoreType.DMA((T + 4,)),
        ],
        compiler_params=pltpu.CompilerParams(
            collective_id=0, has_side_effects=True, vmem_limit_bytes=56 << 20),
        name="rotated_projection",
    )(activations, weight, out_grad.reshape(2, C, tokens, features), had)
    pieces = (1, 1, 8)
    return pl.pallas_call(
        functools.partial(place, pieces),
        out_shape=shapes,
        in_specs=[anywhere] * 3,
        out_specs=(anywhere,) * 3,
        scratch_shapes=[pltpu.SemaphoreType.DMA((sum(pieces),))],
        name="place_results",
    )(*results)


def solution(mesh):
    return jax.shard_map(
        per_device,
        mesh=mesh,
        in_specs=(P("dp", "tensor"), P("tensor", "dp"), P("tensor", "dp")),
        out_specs=(P("tensor", "dp"), P("dp", "tensor"), P("tensor", "dp")),
        check_vma=False,
    )
```

```python
import functools
import math

import jax
import jax.numpy as jnp
import numpy as np
from jax import lax
from jax.experimental import pallas as pl
from jax.experimental.pallas import tpu as pltpu
from jax.sharding import PartitionSpec as P

MESH = pl.DeviceIdType.MESH
YL, Z, C, T, X = 2, 8, 2, 8, 4
LO_CHUNKS = 4
F32, BF16 = jnp.float32, jnp.bfloat16
SEMS = 320


def signs_table(width):
    position = np.arange(width)
    joined = position[:, None] & position[None, :]
    parity = np.zeros_like(joined)
    for bit_number in range(width.bit_length() - 1):
        parity = parity + ((joined >> bit_number) & 1)
    return np.where(parity % 2 == 1, -1.0, 1.0)


def butterfly(parts):
    parts = list(parts)
    apart = 1
    while apart < len(parts):
        for low in range(len(parts)):
            if low & apart == 0:
                a, b = parts[low], parts[low | apart]
                parts[low], parts[low | apart] = a + b, a - b
        apart *= 2
    return parts


def kernel(scale, grad_scale, lo_chunks, act_hbm, w_hbm, og_hbm, had_hbm, out, ing, wg, act, w, og, had,
           w2, s1, x1, s2, r, g, g2, pf, sbp, sbm, rp, rm, ybs, ybr, ys, yr, q, xq, os, oa, t1, v1, t2, igb,
           rg, sems, local_sems):
    d, t = lax.axis_index("dp"), lax.axis_index("tensor")
    c, z, yl = d % C, (d // C) % Z, d // (C * Z)
    yh, x = t // X, t % X
    ahead = 1 - 2 * c
    tokens, width = act.shape
    chunk = width // T
    lo, hi = pl.ds(0, lo_chunks), pl.ds(lo_chunks, T - lo_chunks)

    def block(rel, zz, core):
        return (((yl + rel) % YL) * Z + (zz + 2 * Z) % Z) * C + core

    sib = (block(0, z, 1 - c), t)
    zp, zm = (block(0, z + ahead, c), t), (block(0, z - ahead, c), t)
    yp = (block(1, z, c), t)
    peers = [(d, (t + j) % T) for j in range(1, T)]
    opposite = (d, (t + X) % T)
    along_x = [(d, yh * X + (x + j) % X) for j in range(1, X)]

    barrier = pltpu.get_barrier_semaphore()
    everyone = [sib, zp, zm, yp] + peers
    for other in everyone:
        pl.semaphore_signal(barrier, inc=1, device_id=other, device_id_type=MESH)
    loads = [pltpu.make_async_copy(src, dst, local_sems.at[T + i])
             for i, (src, dst) in enumerate(((act_hbm, act), (had_hbm, had), (og_hbm, og), (w_hbm, w)))]
    for load in loads:
        load.start()
    loads[0].wait()
    loads[1].wait()

    used = [0]
    sent = []

    def pair():
        used[0] += 2
        return used[0] - 2

    def remote(src, dst, to, number):
        return pltpu.make_async_remote_copy(
            src_ref=src, dst_ref=dst, send_sem=sems.at[number], recv_sem=sems.at[number + 1],
            device_id=to, device_id_type=MESH)

    def send(src, dst, to, number):
        copy = remote(src, dst, to, number)
        copy.start()
        sent.append(copy)

    def arrive(dst, number):
        remote(dst, dst, sib, number).wait_recv()

    def local_rotation(parts):
        rows = jnp.concatenate(parts, axis=0)
        table = had[...]
        if rows.dtype == BF16:
            mixed = jnp.dot(rows, table, preferred_element_type=F32)
        else:
            high = rows.astype(BF16)
            rest = rows - high.astype(F32)
            middle = rest.astype(BF16)
            low = (rest - middle.astype(F32)).astype(BF16)
            mixed = (jnp.dot(high, table, preferred_element_type=F32)
                     + jnp.dot(middle, table, preferred_element_type=F32)
                     + jnp.dot(low, table, preferred_element_type=F32))
        return butterfly([mixed[k * tokens:(k + 1) * tokens] for k in range(T)])

    def rotate_first(first, first_in):
        numbers = [pair() for _ in peers]
        for j, peer in enumerate(peers):
            send(first.at[peer[1]], first_in.at[t], peer, numbers[j])
        first_in[t] = first[t]

        def finish():
            for j in range(1, T):
                arrive(first_in.at[(t + T - j) % T], numbers[j - 1])

        return finish

    def rotate_second(first_in, second, landing):
        for k, part in enumerate(butterfly([first_in[k].astype(F32) for k in range(T)])):
            second[k] = (part * scale).astype(BF16)
        numbers = [pair() for _ in peers]
        for j, peer in enumerate(peers):
            send(second.at[peer[1]], landing.at[t], peer, numbers[j])
        landing[t] = second[t]

        def finish():
            for j in range(1, T):
                arrive(landing.at[(t + T - j) % T], numbers[j - 1])

        return finish

    own = block(0, z, c)
    for k, part in enumerate(local_rotation([act[:, k * chunk:(k + 1) * chunk] for k in range(T)])):
        s1[k] = part
    pl.semaphore_wait(barrier, len(everyone))
    first_done = rotate_first(s1, x1)
    loads[2].wait()

    def grad_rows(tt):
        return g.at[pl.ds(2 * tt, 2)]

    opposite_number = pair()
    send(og, grad_rows(t), opposite, opposite_number)
    g[pl.ds(2 * t, 2)] = og[...]
    loads[3].wait()
    w_number = pair()
    send(w, w2, sib, w_number)
    first_done()
    finish = rotate_second(x1, s2, r.at[own])
    near_numbers = [pair() for _ in along_x]
    for j, peer in enumerate(along_x):
        send(og, grad_rows(t), peer, near_numbers[j])
    opposite_t = (t + X) % T
    arrive(grad_rows(opposite_t), opposite_number)
    far_numbers = [pair() for _ in along_x]
    for j, peer in enumerate(along_x):
        send(grad_rows(opposite_t), grad_rows(opposite_t), peer, far_numbers[j])
    finish()

    to_sib = []

    def share(rel, zz, part):
        number = pair()
        send(r.at[block(rel, zz, c), part], r.at[block(rel, zz, c), part], sib, number)
        to_sib.append((block(rel, zz, 1 - c), part, number))

    pieces = ((0, "hi", 1), (1, "lo", 1), (0, "lo", -1))
    halves = {"lo": lo, "hi": hi}
    numbers = {(sign, piece, s): pair() for sign in (1, -1) for piece in pieces for s in range(4)}
    across_numbers = {}

    def pass_on(sign, piece, zz, s):
        view = r.at[block(piece[0], zz, c), halves[piece[1]]]
        send(view, view, zp if sign == 1 else zm, numbers[sign, piece, s])

    def across(zz, step):
        across_numbers[step] = pair()
        view = r.at[block(0, zz, c), hi]
        send(view, view, yp, across_numbers[step])

    def across_arrive(zz, step):
        arrive(r.at[block(1, zz, c), hi], across_numbers[step])
        share(1, zz, hi)

    y_number = pair()
    send(r.at[own, lo], r.at[own, lo], yp, y_number)
    for piece in pieces:
        if piece[0] == 0:
            pass_on(1, piece, z, 0)
            pass_on(-1, piece, z, 0)
    share(0, z, lo)
    share(0, z, hi)
    arrive(r.at[block(1, z, c), lo], y_number)
    pass_on(1, pieces[1], z, 0)
    pass_on(-1, pieces[1], z, 0)
    share(1, z, lo)

    def ring_piece(s, piece):
        rel, half, far = piece
        for sign in (1, -1):
            if s == 3 and sign != far:
                continue
            zz = z - sign * ahead * (1 + s)
            arrive(r.at[block(rel, zz, c), halves[half]], numbers[sign, piece, s])
            if s < 2 or (s == 2 and sign == far):
                pass_on(sign, piece, zz, s + 1)
            share(rel, zz, halves[half])

    def ring_step(s):
        for piece in pieces:
            ring_piece(s, piece)

    def across_send(s):
        for sign in (1, -1):
            if s < 3 or sign == 1:
                across(z - sign * ahead * (1 + s), sign * (1 + s))

    def across_step(s):
        for sign in (1, -1):
            if s < 3 or sign == 1:
                across_arrive(z - sign * ahead * (1 + s), sign * (1 + s))

    ring_piece(0, pieces[0])
    ring_piece(0, pieces[2])
    for j in range(1, X):
        from_x = (x + X - j) % X
        arrive(grad_rows(yh * X + from_x), near_numbers[j - 1])
        arrive(grad_rows((1 - yh) * X + from_x), far_numbers[j - 1])
    g2_number = pair()
    send(g.at[:, 1 - c], g2, sib, g2_number)
    ring_piece(0, pieces[1])
    arrive(g2, g2_number)
    arrive(w2, w_number)

    rows = Z * YL * tokens

    def partial(k, carry):
        mine = g[:, c].reshape(rows, g.shape[-1])
        theirs = g2[...].reshape(rows, g.shape[-1])
        at = pl.ds(pl.multiple_of(k * chunk, chunk), chunk)
        dims = (((1,), (1,)), ((), ()))
        total = (lax.dot_general(mine, w[at, :], dims, preferred_element_type=F32)
                 + lax.dot_general(theirs, w2[at, :], dims, preferred_element_type=F32))
        pf[:, k] = total.reshape(Z * YL, tokens, chunk)
        return carry

    sums = {(sign, piece, s): pair() for sign in (1, -1) for piece in pieces for s in range(4)}
    back_numbers = {}

    def target(rel, zz):
        return block(rel, zz, 0) // C

    def give_across(away):
        i = away + 4
        ybs[i] = pf[target(1, z + ahead * away), hi].astype(BF16)
        back_numbers[away] = pair()
        send(ybs.at[i], ybr.at[i], yp, back_numbers[away])

    def reduce_piece(s, piece):
        rel, half, far = piece
        part = halves[half]
        for sign in (1, -1):
            if s == 0 and sign != far:
                continue
            into, out_of, to = (rp, sbp, zp) if sign == 1 else (rm, sbm, zm)
            away = sign * (4 - s)
            total = pf[target(rel, z + ahead * away), part]
            if half == "hi":
                arrive(ybr.at[away + 4], back_numbers[away])
                total = total + ybr[away + 4].astype(F32)
            if s > 1 or (s == 1 and sign == far):
                arrive(into.at[rel, s - 1, part], sums[sign, piece, s - 1])
                total = total + into[rel, s - 1, part].astype(F32)
            out_of[rel, s, part] = total.astype(BF16)
            send(out_of.at[rel, s, part], into.at[rel, s, part], to, sums[sign, piece, s])

    order = (pieces[1], pieces[2], pieces[0])

    def reduce_step(s):
        for piece in order:
            reduce_piece(s, piece)

    lax.fori_loop(lo_chunks, T, partial, 0)
    for away in (4, 3, -3, 2, -2, 1, -1, 0):
        give_across(away)
    lax.fori_loop(0, lo_chunks, partial, 0)
    reduce_piece(0, order[0])
    reduce_piece(0, order[1])
    ring_step(1)
    reduce_piece(0, order[2])
    across(z, 0)
    across_send(0)
    reduce_step(1)
    ring_step(2)
    across_send(1)
    across_send(2)
    reduce_step(2)
    ring_step(3)
    across_send(3)
    across_arrive(z, 0)
    across_step(0)
    reduce_step(3)
    across_step(1)
    across_step(2)

    def products(i, carry):
        total = jnp.zeros((256, w.shape[1]), F32)
        for k in range(T):
            lhs = r[pl.ds(8 * i, 8), k].reshape(256, chunk)
            total = total + jnp.dot(lhs, w[k * chunk:(k + 1) * chunk, :], preferred_element_type=F32)
        q[i // 2, pl.ds(2 * (i % 2), 2)] = total.reshape(2, 128, w.shape[1]).astype(BF16)
        return carry

    def weight_grad(k, carry):
        lhs = r[:, k].reshape(2 * rows, chunk)
        rhs = g[...].reshape(2 * rows, g.shape[-1])
        total = lax.dot_general(lhs, rhs, (((0,), (0,)), ((), ())), preferred_element_type=F32)
        at = pl.ds(pl.multiple_of(k * chunk, chunk), chunk)
        wg[at, :] = total * grad_scale
        return carry

    across_step(3)
    for b, part, number in to_sib:
        arrive(r.at[b, part], number)
    lax.fori_loop(0, 4, products, 0)
    out_numbers = [pair() for _ in along_x]
    for j, peer in enumerate(along_x):
        send(q.at[:, (x + j + 1) % X], xq.at[x], peer, out_numbers[j])
    xq[x] = q[:, x]
    lax.fori_loop(0, 3, weight_grad, 0)

    def finals(piece):
        rel, half, far = piece
        part = halves[half]
        total = pf[target(rel, z), part]
        for sign, into in ((1, rp), (-1, rm)):
            arrive(into.at[rel, 3, part], sums[sign, piece, 3])
            total = total + into[rel, 3, part].astype(F32)
        return total

    ys[...] = finals(order[0]).astype(BF16)
    back_number = pair()
    send(ys, yr, yp, back_number)
    rg[lo] = finals(order[1])
    arrive(ybr.at[4], back_numbers[0])
    rg[hi] = finals(order[2]) + ybr[4].astype(F32)
    lax.fori_loop(3, 5, weight_grad, 0)
    arrive(yr, back_number)
    rg[lo] = rg[lo] + yr[...].astype(F32)
    for k, part in enumerate(local_rotation([rg[k] for k in range(T)])):
        t1[k] = part.astype(BF16)
    first_done = rotate_first(t1, v1)
    lax.fori_loop(5, 8, weight_grad, 0)
    first_done()
    finish = rotate_second(v1, t2, igb)

    def out_sum(half):
        total = xq[0, half].astype(F32)
        for k in range(1, X):
            total = total + xq[k, half].astype(F32)
        return total

    for j in range(1, X):
        arrive(xq.at[(x + X - j) % X], out_numbers[j - 1])
    os[...] = out_sum(1 - yh).astype(BF16)
    last_number = pair()
    send(os, oa, opposite, last_number)
    total = out_sum(yh)
    arrive(oa, last_number)
    out[...] = (total + oa[...].astype(F32)).astype(BF16)

    finish()
    for k in range(T):
        ing[:, k * chunk:(k + 1) * chunk] = igb[k]

    for copy in sent:
        copy.wait_send()

    assert used[0] <= SEMS, used[0]


def place(out_in, ing_in, wg_in, out, ing, wg, sems):
    rows = wg.shape[0] // T
    copies = [pltpu.make_async_copy(out_in, out, sems.at[T]),
              pltpu.make_async_copy(ing_in, ing, sems.at[T + 1])]
    for i in range(T):
        at = pl.ds(i * rows, rows)
        copies.append(pltpu.make_async_copy(wg_in.at[at], wg.at[at], sems.at[i]))
    for copy in copies:
        copy.start()
    for copy in copies:
        copy.wait()


def per_device(activations, weight, out_grad):
    tokens, width = activations.shape
    features = weight.shape[1]
    groups = YL * Z * C
    chunk = width // T
    scale = 1.0 / math.sqrt(width * T)
    grad_scale = 1.0 / math.sqrt(tokens * groups)
    had = jnp.asarray(signs_table(chunk), BF16)
    vmem = pl.BlockSpec(memory_space=pltpu.VMEM)
    anywhere = pl.BlockSpec(memory_space=pl.ANY)
    part = (T, tokens, chunk)
    low = (LO_CHUNKS, tokens, chunk)
    high = (T - LO_CHUNKS, tokens, chunk)
    shapes = (
        jax.ShapeDtypeStruct((out_grad.shape[0], features), BF16),
        jax.ShapeDtypeStruct((tokens, width), BF16),
        jax.ShapeDtypeStruct((width, features), F32),
    )
    results = pl.pallas_call(
        functools.partial(kernel, scale, grad_scale, LO_CHUNKS),
        out_shape=tuple(pltpu.VMEM(leaf.shape, leaf.dtype) for leaf in shapes),
        in_specs=[pl.BlockSpec(memory_space=pltpu.HBM)] * 4,
        out_specs=(vmem,) * 3,
        scratch_shapes=[
            pltpu.VMEM((tokens, width), BF16),
            pltpu.VMEM((width, features), BF16),
            pltpu.VMEM((2, C, tokens, features), BF16),
            pltpu.VMEM((chunk, chunk), BF16),
            pltpu.VMEM((width, features), BF16),
            pltpu.VMEM(part, F32), pltpu.VMEM(part, F32), pltpu.VMEM(part, BF16),
            pltpu.VMEM((groups,) + part, BF16),
            pltpu.VMEM((groups // C, C, tokens, features), BF16),
            pltpu.VMEM((groups // C, tokens, features), BF16),
            pltpu.VMEM((groups // C,) + part, F32),
            pltpu.VMEM((2, 4) + part, BF16), pltpu.VMEM((2, 4) + part, BF16),
            pltpu.VMEM((2, 4) + part, BF16), pltpu.VMEM((2, 4) + part, BF16),
            pltpu.VMEM((9,) + high, BF16), pltpu.VMEM((9,) + high, BF16),
            pltpu.VMEM(low, BF16), pltpu.VMEM(low, BF16),
            pltpu.VMEM((T // X, X, out_grad.shape[0], features), BF16),
            pltpu.VMEM((X, T // X, out_grad.shape[0], features), BF16),
            pltpu.VMEM((out_grad.shape[0], features), BF16),
            pltpu.VMEM((out_grad.shape[0], features), BF16),
            pltpu.VMEM(part, BF16), pltpu.VMEM(part, BF16),
            pltpu.VMEM(part, BF16), pltpu.VMEM(part, BF16),
                pltpu.VMEM(part, F32),
            pltpu.SemaphoreType.DMA((SEMS,)),
            pltpu.SemaphoreType.DMA((T + 4,)),
        ],
        compiler_params=pltpu.CompilerParams(
            collective_id=0, has_side_effects=True, vmem_limit_bytes=237 << 18),
        name="rotated_projection",
    )(activations, weight, out_grad.reshape(2, C, tokens, features), had)
    return pl.pallas_call(
        place,
        out_shape=shapes,
        in_specs=[vmem] * 3,
        out_specs=(anywhere,) * 3,
        scratch_shapes=[pltpu.SemaphoreType.DMA((T + 2,))],
        compiler_params=pltpu.CompilerParams(vmem_limit_bytes=16 << 20),
        name="place_results",
    )(*results)


def solution(mesh):
    return jax.shard_map(
        per_device,
        mesh=mesh,
        in_specs=(P("dp", "tensor"), P("tensor", "dp"), P("tensor", "dp")),
        out_specs=(P("tensor", "dp"), P("dp", "tensor"), P("tensor", "dp")),
        check_vma=False,
    )
```

```python
import functools
import math

import jax
import jax.numpy as jnp
import numpy as np
from jax import lax
from jax.experimental import pallas as pl
from jax.experimental.pallas import tpu as pltpu
from jax.sharding import PartitionSpec as P

MESH = pl.DeviceIdType.MESH
YL, Z, C, T, X = 2, 8, 2, 8, 4
LO_CHUNKS = 5
F32, BF16 = jnp.float32, jnp.bfloat16
SEMS = 320


def signs_table(width):
    position = np.arange(width)
    joined = position[:, None] & position[None, :]
    parity = np.zeros_like(joined)
    for bit_number in range(width.bit_length() - 1):
        parity = parity + ((joined >> bit_number) & 1)
    return np.where(parity % 2 == 1, -1.0, 1.0)


def butterfly(parts):
    parts = list(parts)
    apart = 1
    while apart < len(parts):
        for low in range(len(parts)):
            if low & apart == 0:
                a, b = parts[low], parts[low | apart]
                parts[low], parts[low | apart] = a + b, a - b
        apart *= 2
    return parts


def kernel(scale, grad_scale, lo_chunks, act_hbm, w_hbm, og_hbm, had_hbm, out, ing, wg, act, w, og, had,
           w2, s1, x1, s2, r, g, g2, pf, sbp, sbm, rp, rm, ybs, ybr, ys, yr, q, xq, os, oa, t1, v1, t2, igb,
           rg, sems, local_sems):
    d, t = lax.axis_index("dp"), lax.axis_index("tensor")
    c, z, yl = d % C, (d // C) % Z, d // (C * Z)
    yh, x = t // X, t % X
    ahead = 1 - 2 * c
    tokens, width = act.shape
    chunk = width // T
    lo, hi = pl.ds(0, lo_chunks), pl.ds(lo_chunks, T - lo_chunks)

    def block(rel, zz, core):
        return (((yl + rel) % YL) * Z + (zz + 2 * Z) % Z) * C + core

    sib = (block(0, z, 1 - c), t)
    zp, zm = (block(0, z + ahead, c), t), (block(0, z - ahead, c), t)
    yp = (block(1, z, c), t)
    peers = [(d, (t + j) % T) for j in range(1, T)]
    opposite = (d, (t + X) % T)
    along_x = [(d, yh * X + (x + j) % X) for j in range(1, X)]

    barrier = pltpu.get_barrier_semaphore()
    everyone = [sib, zp, zm, yp] + peers
    for other in everyone:
        pl.semaphore_signal(barrier, inc=1, device_id=other, device_id_type=MESH)
    loads = [pltpu.make_async_copy(src, dst, local_sems.at[T + i])
             for i, (src, dst) in enumerate(((act_hbm, act), (had_hbm, had), (og_hbm, og), (w_hbm, w)))]
    for load in loads:
        load.start()
    loads[0].wait()
    loads[1].wait()

    used = [0]
    sent = []

    def pair():
        used[0] += 2
        return used[0] - 2

    def remote(src, dst, to, number):
        return pltpu.make_async_remote_copy(
            src_ref=src, dst_ref=dst, send_sem=sems.at[number], recv_sem=sems.at[number + 1],
            device_id=to, device_id_type=MESH)

    def send(src, dst, to, number):
        copy = remote(src, dst, to, number)
        copy.start()
        sent.append(copy)

    def arrive(dst, number):
        remote(dst, dst, sib, number).wait_recv()

    def local_rotation(parts):
        rows = jnp.concatenate(parts, axis=0)
        table = had[...]
        if rows.dtype == BF16:
            mixed = jnp.dot(rows, table, preferred_element_type=F32)
        else:
            high = rows.astype(BF16)
            rest = rows - high.astype(F32)
            middle = rest.astype(BF16)
            low = (rest - middle.astype(F32)).astype(BF16)
            mixed = (jnp.dot(high, table, preferred_element_type=F32)
                     + jnp.dot(middle, table, preferred_element_type=F32)
                     + jnp.dot(low, table, preferred_element_type=F32))
        return butterfly([mixed[k * tokens:(k + 1) * tokens] for k in range(T)])

    def rotate_first(first, first_in):
        numbers = [pair() for _ in peers]
        for j, peer in enumerate(peers):
            send(first.at[peer[1]], first_in.at[t], peer, numbers[j])
        first_in[t] = first[t]

        def finish():
            for j in range(1, T):
                arrive(first_in.at[(t + T - j) % T], numbers[j - 1])

        return finish

    def rotate_second(first_in, second, landing):
        for k, part in enumerate(butterfly([first_in[k].astype(F32) for k in range(T)])):
            second[k] = (part * scale).astype(BF16)
        numbers = [pair() for _ in peers]
        for j, peer in enumerate(peers):
            send(second.at[peer[1]], landing.at[t], peer, numbers[j])
        landing[t] = second[t]

        def finish():
            for j in range(1, T):
                arrive(landing.at[(t + T - j) % T], numbers[j - 1])

        return finish

    own = block(0, z, c)
    for k, part in enumerate(local_rotation([act[:, k * chunk:(k + 1) * chunk] for k in range(T)])):
        s1[k] = part
    pl.semaphore_wait(barrier, len(everyone))
    first_done = rotate_first(s1, x1)
    loads[2].wait()

    def grad_rows(tt):
        return g.at[pl.ds(2 * tt, 2)]

    opposite_number = pair()
    send(og, grad_rows(t), opposite, opposite_number)
    g[pl.ds(2 * t, 2)] = og[...]
    loads[3].wait()
    w_number = pair()
    send(w, w2, sib, w_number)
    first_done()
    finish = rotate_second(x1, s2, r.at[own])
    near_numbers = [pair() for _ in along_x]
    for j, peer in enumerate(along_x):
        send(og, grad_rows(t), peer, near_numbers[j])
    opposite_t = (t + X) % T
    arrive(grad_rows(opposite_t), opposite_number)
    far_numbers = [pair() for _ in along_x]
    for j, peer in enumerate(along_x):
        send(grad_rows(opposite_t), grad_rows(opposite_t), peer, far_numbers[j])
    finish()

    to_sib = []

    def share(rel, zz, part):
        number = pair()
        send(r.at[block(rel, zz, c), part], r.at[block(rel, zz, c), part], sib, number)
        to_sib.append((block(rel, zz, 1 - c), part, number))

    pieces = ((0, "hi", 1), (1, "lo", 1), (0, "lo", -1))
    halves = {"lo": lo, "hi": hi}
    numbers = {(sign, piece, s): pair() for sign in (1, -1) for piece in pieces for s in range(4)}
    across_numbers = {}

    def pass_on(sign, piece, zz, s):
        view = r.at[block(piece[0], zz, c), halves[piece[1]]]
        send(view, view, zp if sign == 1 else zm, numbers[sign, piece, s])

    def across(zz, step):
        across_numbers[step] = pair()
        view = r.at[block(0, zz, c), hi]
        send(view, view, yp, across_numbers[step])

    def across_arrive(zz, step):
        arrive(r.at[block(1, zz, c), hi], across_numbers[step])
        share(1, zz, hi)

    y_number = pair()
    send(r.at[own, lo], r.at[own, lo], yp, y_number)
    for piece in pieces:
        if piece[0] == 0:
            pass_on(1, piece, z, 0)
            pass_on(-1, piece, z, 0)
    share(0, z, lo)
    share(0, z, hi)
    arrive(r.at[block(1, z, c), lo], y_number)
    pass_on(1, pieces[1], z, 0)
    pass_on(-1, pieces[1], z, 0)
    across(z, 0)
    share(1, z, lo)

    def ring_piece(s, piece):
        rel, half, far = piece
        for sign in (1, -1):
            if s == 3 and sign != far:
                continue
            zz = z - sign * ahead * (1 + s)
            arrive(r.at[block(rel, zz, c), halves[half]], numbers[sign, piece, s])
            if s < 2 or (s == 2 and sign == far):
                pass_on(sign, piece, zz, s + 1)
            if rel == 0 and half == "hi":
                across(zz, sign * (1 + s))
            share(rel, zz, halves[half])

    def ring_step(s):
        for piece in pieces:
            ring_piece(s, piece)

    def across_step(s):
        for sign in (1, -1):
            if s < 3 or sign == 1:
                across_arrive(z - sign * ahead * (1 + s), sign * (1 + s))

    ring_step(0)
    for j in range(1, X):
        from_x = (x + X - j) % X
        arrive(grad_rows(yh * X + from_x), near_numbers[j - 1])
        arrive(grad_rows((1 - yh) * X + from_x), far_numbers[j - 1])
    g2_number = pair()
    send(g.at[:, 1 - c], g2, sib, g2_number)
    across_arrive(z, 0)
    ring_step(1)
    arrive(g2, g2_number)
    arrive(w2, w_number)

    rows = Z * YL * tokens

    def partial(k, carry):
        mine = g[:, c].reshape(rows, g.shape[-1])
        theirs = g2[...].reshape(rows, g.shape[-1])
        at = pl.ds(pl.multiple_of(k * chunk, chunk), chunk)
        dims = (((1,), (1,)), ((), ()))
        total = (lax.dot_general(mine, w[at, :], dims, preferred_element_type=F32)
                 + lax.dot_general(theirs, w2[at, :], dims, preferred_element_type=F32))
        pf[:, k] = total.reshape(Z * YL, tokens, chunk)
        return carry

    sums = {(sign, piece, s): pair() for sign in (1, -1) for piece in pieces for s in range(4)}
    back_numbers = {}

    def target(rel, zz):
        return block(rel, zz, 0) // C

    def give_across(away):
        i = away + 4
        ybs[i] = pf[target(1, z + ahead * away), hi].astype(BF16)
        back_numbers[away] = pair()
        send(ybs.at[i], ybr.at[i], yp, back_numbers[away])

    def reduce_piece(s, piece):
        rel, half, far = piece
        part = halves[half]
        for sign in (1, -1):
            if s == 0 and sign != far:
                continue
            into, out_of, to = (rp, sbp, zp) if sign == 1 else (rm, sbm, zm)
            away = sign * (4 - s)
            total = pf[target(rel, z + ahead * away), part]
            if half == "hi":
                arrive(ybr.at[away + 4], back_numbers[away])
                total = total + ybr[away + 4].astype(F32)
            if s > 1 or (s == 1 and sign == far):
                arrive(into.at[rel, s - 1, part], sums[sign, piece, s - 1])
                total = total + into[rel, s - 1, part].astype(F32)
            out_of[rel, s, part] = total.astype(BF16)
            send(out_of.at[rel, s, part], into.at[rel, s, part], to, sums[sign, piece, s])

    order = (pieces[1], pieces[2], pieces[0])

    def reduce_step(s):
        for piece in order:
            reduce_piece(s, piece)

    lax.fori_loop(0, lo_chunks, partial, 0)
    reduce_piece(0, order[0])
    reduce_piece(0, order[1])
    lax.fori_loop(lo_chunks, T, partial, 0)
    across_step(0)
    ring_step(2)
    for away in (4, 3, -3, 2, -2, 1, -1, 0):
        give_across(away)
    across_step(1)
    ring_step(3)
    reduce_piece(0, order[2])
    reduce_step(1)
    across_step(2)

    def products(i, carry):
        total = jnp.zeros((256, w.shape[1]), F32)
        for k in range(T):
            lhs = r[pl.ds(8 * i, 8), k].reshape(256, chunk)
            total = total + jnp.dot(lhs, w[k * chunk:(k + 1) * chunk, :], preferred_element_type=F32)
        q[i // 2, pl.ds(2 * (i % 2), 2)] = total.reshape(2, 128, w.shape[1]).astype(BF16)
        return carry

    def weight_grad(k, carry):
        lhs = r[:, k].reshape(2 * rows, chunk)
        rhs = g[...].reshape(2 * rows, g.shape[-1])
        total = lax.dot_general(lhs, rhs, (((0,), (0,)), ((), ())), preferred_element_type=F32)
        at = pl.ds(pl.multiple_of(k * chunk, chunk), chunk)
        wg[at, :] = total * grad_scale
        return carry

    across_step(3)
    for b, part, number in to_sib:
        arrive(r.at[b, part], number)
    lax.fori_loop(0, 4, products, 0)
    out_numbers = [pair() for _ in along_x]
    for j, peer in enumerate(along_x):
        send(q.at[:, (x + j + 1) % X], xq.at[x], peer, out_numbers[j])
    xq[x] = q[:, x]
    reduce_step(2)
    lax.fori_loop(0, 3, weight_grad, 0)
    reduce_step(3)

    def finals(piece):
        rel, half, far = piece
        part = halves[half]
        total = pf[target(rel, z), part]
        for sign, into in ((1, rp), (-1, rm)):
            arrive(into.at[rel, 3, part], sums[sign, piece, 3])
            total = total + into[rel, 3, part].astype(F32)
        return total

    ys[...] = finals(order[0]).astype(BF16)
    back_number = pair()
    send(ys, yr, yp, back_number)
    rg[lo] = finals(order[1])
    arrive(ybr.at[4], back_numbers[0])
    rg[hi] = finals(order[2]) + ybr[4].astype(F32)
    lax.fori_loop(3, 5, weight_grad, 0)
    arrive(yr, back_number)
    rg[lo] = rg[lo] + yr[...].astype(F32)
    for k, part in enumerate(local_rotation([rg[k] for k in range(T)])):
        t1[k] = part.astype(BF16)
    first_done = rotate_first(t1, v1)

    def out_sum(half):
        total = xq[0, half].astype(F32)
        for k in range(1, X):
            total = total + xq[k, half].astype(F32)
        return total

    for j in range(1, X):
        arrive(xq.at[(x + X - j) % X], out_numbers[j - 1])
    os[...] = out_sum(1 - yh).astype(BF16)
    last_number = pair()
    send(os, oa, opposite, last_number)
    first_done()
    finish = rotate_second(v1, t2, igb)
    lax.fori_loop(5, 8, weight_grad, 0)
    total = out_sum(yh)
    arrive(oa, last_number)
    out[...] = (total + oa[...].astype(F32)).astype(BF16)

    finish()
    for k in range(T):
        ing[:, k * chunk:(k + 1) * chunk] = igb[k]

    for copy in sent:
        copy.wait_send()

    assert used[0] <= SEMS, used[0]


def place(out_in, ing_in, wg_in, out, ing, wg, sems):
    rows = wg.shape[0] // T
    copies = [pltpu.make_async_copy(out_in, out, sems.at[T]),
              pltpu.make_async_copy(ing_in, ing, sems.at[T + 1])]
    for i in range(T):
        at = pl.ds(i * rows, rows)
        copies.append(pltpu.make_async_copy(wg_in.at[at], wg.at[at], sems.at[i]))
    for copy in copies:
        copy.start()
    for copy in copies:
        copy.wait()


def per_device(activations, weight, out_grad):
    tokens, width = activations.shape
    features = weight.shape[1]
    groups = YL * Z * C
    chunk = width // T
    scale = 1.0 / math.sqrt(width * T)
    grad_scale = 1.0 / math.sqrt(tokens * groups)
    had = jnp.asarray(signs_table(chunk), BF16)
    vmem = pl.BlockSpec(memory_space=pltpu.VMEM)
    anywhere = pl.BlockSpec(memory_space=pl.ANY)
    part = (T, tokens, chunk)
    low = (LO_CHUNKS, tokens, chunk)
    high = (T - LO_CHUNKS, tokens, chunk)
    shapes = (
        jax.ShapeDtypeStruct((out_grad.shape[0], features), BF16),
        jax.ShapeDtypeStruct((tokens, width), BF16),
        jax.ShapeDtypeStruct((width, features), F32),
    )
    results = pl.pallas_call(
        functools.partial(kernel, scale, grad_scale, LO_CHUNKS),
        out_shape=tuple(pltpu.VMEM(leaf.shape, leaf.dtype) for leaf in shapes),
        in_specs=[pl.BlockSpec(memory_space=pltpu.HBM)] * 4,
        out_specs=(vmem,) * 3,
        scratch_shapes=[
            pltpu.VMEM((tokens, width), BF16),
            pltpu.VMEM((width, features), BF16),
            pltpu.VMEM((2, C, tokens, features), BF16),
            pltpu.VMEM((chunk, chunk), BF16),
            pltpu.VMEM((width, features), BF16),
            pltpu.VMEM(part, F32), pltpu.VMEM(part, F32), pltpu.VMEM(part, BF16),
            pltpu.VMEM((groups,) + part, BF16),
            pltpu.VMEM((groups // C, C, tokens, features), BF16),
            pltpu.VMEM((groups // C, tokens, features), BF16),
            pltpu.VMEM((groups // C,) + part, F32),
            pltpu.VMEM((2, 4) + part, BF16), pltpu.VMEM((2, 4) + part, BF16),
            pltpu.VMEM((2, 4) + part, BF16), pltpu.VMEM((2, 4) + part, BF16),
            pltpu.VMEM((9,) + high, BF16), pltpu.VMEM((9,) + high, BF16),
            pltpu.VMEM(low, BF16), pltpu.VMEM(low, BF16),
            pltpu.VMEM((T // X, X, out_grad.shape[0], features), BF16),
            pltpu.VMEM((X, T // X, out_grad.shape[0], features), BF16),
            pltpu.VMEM((out_grad.shape[0], features), BF16),
            pltpu.VMEM((out_grad.shape[0], features), BF16),
            pltpu.VMEM(part, BF16), pltpu.VMEM(part, BF16),
            pltpu.VMEM(part, BF16), pltpu.VMEM(part, BF16),
                pltpu.VMEM(part, F32),
            pltpu.SemaphoreType.DMA((SEMS,)),
            pltpu.SemaphoreType.DMA((T + 4,)),
        ],
        compiler_params=pltpu.CompilerParams(
            collective_id=0, has_side_effects=True, vmem_limit_bytes=237 << 18),
        name="rotated_projection",
    )(activations, weight, out_grad.reshape(2, C, tokens, features), had)
    return pl.pallas_call(
        place,
        out_shape=shapes,
        in_specs=[vmem] * 3,
        out_specs=(anywhere,) * 3,
        scratch_shapes=[pltpu.SemaphoreType.DMA((T + 2,))],
        compiler_params=pltpu.CompilerParams(vmem_limit_bytes=16 << 20),
        name="place_results",
    )(*results)


def solution(mesh):
    return jax.shard_map(
        per_device,
        mesh=mesh,
        in_specs=(P("dp", "tensor"), P("tensor", "dp"), P("tensor", "dp")),
        out_specs=(P("tensor", "dp"), P("dp", "tensor"), P("tensor", "dp")),
        check_vma=False,
    )
```

```python
import functools
import math

import jax
import jax.numpy as jnp
import numpy as np
from jax import lax
from jax.experimental import pallas as pl
from jax.experimental.pallas import tpu as pltpu
from jax.sharding import PartitionSpec as P

MESH = pl.DeviceIdType.MESH
YL, Z, C, T, X = 2, 8, 2, 8, 4
LO_CHUNKS = 4
SUM_CHUNKS = 6
F32, BF16 = jnp.float32, jnp.bfloat16
SEMS = 320


def signs_table(width):
    position = np.arange(width)
    joined = position[:, None] & position[None, :]
    parity = np.zeros_like(joined)
    for bit_number in range(width.bit_length() - 1):
        parity = parity + ((joined >> bit_number) & 1)
    return np.where(parity % 2 == 1, -1.0, 1.0)


def butterfly(parts):
    parts = list(parts)
    apart = 1
    while apart < len(parts):
        for low in range(len(parts)):
            if low & apart == 0:
                a, b = parts[low], parts[low | apart]
                parts[low], parts[low | apart] = a + b, a - b
        apart *= 2
    return parts


def kernel(scale, grad_scale, lo_chunks, sum_chunks, act_hbm, w_hbm, og_hbm, had_hbm, out, ing, wg, act, w, og, had,
           w2, s1, x1, s2, r, g, g2, pf, sbp, sbm, rp, rm, ybs, ybr, ys, yr, q, xq, os, oa, t1, v1, t2, igb,
           rg, sems, local_sems):
    d, t = lax.axis_index("dp"), lax.axis_index("tensor")
    c, z, yl = d % C, (d // C) % Z, d // (C * Z)
    yh, x = t // X, t % X
    ahead = 1 - 2 * c
    tokens, width = act.shape
    chunk = width // T
    lo, hi = pl.ds(0, lo_chunks), pl.ds(lo_chunks, T - lo_chunks)

    def block(rel, zz, core):
        return (((yl + rel) % YL) * Z + (zz + 2 * Z) % Z) * C + core

    sib = (block(0, z, 1 - c), t)
    zp, zm = (block(0, z + ahead, c), t), (block(0, z - ahead, c), t)
    yp = (block(1, z, c), t)
    peers = [(d, (t + j) % T) for j in range(1, T)]
    opposite = (d, (t + X) % T)
    along_x = [(d, yh * X + (x + j) % X) for j in range(1, X)]

    barrier = pltpu.get_barrier_semaphore()
    everyone = [sib, zp, zm, yp] + peers
    for other in everyone:
        pl.semaphore_signal(barrier, inc=1, device_id=other, device_id_type=MESH)
    loads = [pltpu.make_async_copy(src, dst, local_sems.at[T + i])
             for i, (src, dst) in enumerate(((act_hbm, act), (had_hbm, had), (og_hbm, og), (w_hbm, w)))]
    for load in loads:
        load.start()
    loads[0].wait()
    loads[1].wait()

    used = [0]
    sent = []

    def pair():
        used[0] += 2
        return used[0] - 2

    def remote(src, dst, to, number):
        return pltpu.make_async_remote_copy(
            src_ref=src, dst_ref=dst, send_sem=sems.at[number], recv_sem=sems.at[number + 1],
            device_id=to, device_id_type=MESH)

    def send(src, dst, to, number):
        copy = remote(src, dst, to, number)
        copy.start()
        sent.append(copy)

    def arrive(dst, number):
        remote(dst, dst, sib, number).wait_recv()

    def local_rotation(parts):
        rows = jnp.concatenate(parts, axis=0)
        table = had[...]
        if rows.dtype == BF16:
            mixed = jnp.dot(rows, table, preferred_element_type=F32)
        else:
            high = rows.astype(BF16)
            rest = rows - high.astype(F32)
            middle = rest.astype(BF16)
            low = (rest - middle.astype(F32)).astype(BF16)
            mixed = (jnp.dot(high, table, preferred_element_type=F32)
                     + jnp.dot(middle, table, preferred_element_type=F32)
                     + jnp.dot(low, table, preferred_element_type=F32))
        return butterfly([mixed[k * tokens:(k + 1) * tokens] for k in range(T)])

    def rotate_first(first, first_in):
        numbers = [pair() for _ in peers]
        for j, peer in enumerate(peers):
            send(first.at[peer[1]], first_in.at[t], peer, numbers[j])
        first_in[t] = first[t]

        def finish():
            for j in range(1, T):
                arrive(first_in.at[(t + T - j) % T], numbers[j - 1])

        return finish

    def rotate_second(first_in, second, landing):
        for k, part in enumerate(butterfly([first_in[k].astype(F32) for k in range(T)])):
            second[k] = (part * scale).astype(BF16)
        numbers = [pair() for _ in peers]
        for j, peer in enumerate(peers):
            send(second.at[peer[1]], landing.at[t], peer, numbers[j])
        landing[t] = second[t]

        def finish():
            for j in range(1, T):
                arrive(landing.at[(t + T - j) % T], numbers[j - 1])

        return finish

    own = block(0, z, c)
    for k, part in enumerate(local_rotation([act[:, k * chunk:(k + 1) * chunk] for k in range(T)])):
        s1[k] = part
    pl.semaphore_wait(barrier, len(everyone))
    first_done = rotate_first(s1, x1)
    loads[2].wait()

    def grad_rows(tt):
        return g.at[pl.ds(2 * tt, 2)]

    opposite_number = pair()
    send(og, grad_rows(t), opposite, opposite_number)
    g[pl.ds(2 * t, 2)] = og[...]
    loads[3].wait()
    w_number = pair()
    send(w, w2, sib, w_number)
    first_done()
    finish = rotate_second(x1, s2, r.at[own])
    near_numbers = [pair() for _ in along_x]
    for j, peer in enumerate(along_x):
        send(og, grad_rows(t), peer, near_numbers[j])
    opposite_t = (t + X) % T
    arrive(grad_rows(opposite_t), opposite_number)
    far_numbers = [pair() for _ in along_x]
    for j, peer in enumerate(along_x):
        send(grad_rows(opposite_t), grad_rows(opposite_t), peer, far_numbers[j])
    finish()

    to_sib = []

    def share(rel, zz, part):
        number = pair()
        send(r.at[block(rel, zz, c), part], r.at[block(rel, zz, c), part], sib, number)
        to_sib.append((block(rel, zz, 1 - c), part, number))

    pieces = ((0, "hi", 1), (1, "lo", 1), (0, "lo", -1))
    halves = {"lo": lo, "hi": hi}
    numbers = {(sign, piece, s): pair() for sign in (1, -1) for piece in pieces for s in range(4)}
    across_numbers = {}

    def pass_on(sign, piece, zz, s):
        view = r.at[block(piece[0], zz, c), halves[piece[1]]]
        send(view, view, zp if sign == 1 else zm, numbers[sign, piece, s])

    def across(zz, step):
        across_numbers[step] = pair()
        view = r.at[block(0, zz, c), hi]
        send(view, view, yp, across_numbers[step])

    def across_arrive(zz, step):
        arrive(r.at[block(1, zz, c), hi], across_numbers[step])
        share(1, zz, hi)

    y_number = pair()
    send(r.at[own, lo], r.at[own, lo], yp, y_number)
    for piece in pieces:
        if piece[0] == 0:
            pass_on(1, piece, z, 0)
            pass_on(-1, piece, z, 0)
    share(0, z, lo)
    share(0, z, hi)
    arrive(r.at[block(1, z, c), lo], y_number)
    pass_on(1, pieces[1], z, 0)
    pass_on(-1, pieces[1], z, 0)
    across(z, 0)
    share(1, z, lo)

    def ring_piece(s, piece):
        rel, half, far = piece
        for sign in (1, -1):
            if s == 3 and sign != far:
                continue
            zz = z - sign * ahead * (1 + s)
            arrive(r.at[block(rel, zz, c), halves[half]], numbers[sign, piece, s])
            if s < 2 or (s == 2 and sign == far):
                pass_on(sign, piece, zz, s + 1)
            if rel == 0 and half == "hi":
                across(zz, sign * (1 + s))
            share(rel, zz, halves[half])

    def ring_step(s):
        for piece in pieces:
            ring_piece(s, piece)

    def across_step(s):
        for sign in (1, -1):
            if s < 3 or sign == 1:
                across_arrive(z - sign * ahead * (1 + s), sign * (1 + s))

    ring_step(0)
    for j in range(1, X):
        from_x = (x + X - j) % X
        arrive(grad_rows(yh * X + from_x), near_numbers[j - 1])
        arrive(grad_rows((1 - yh) * X + from_x), far_numbers[j - 1])
    g2_number = pair()
    send(g.at[:, 1 - c], g2, sib, g2_number)
    across_arrive(z, 0)
    ring_step(1)
    arrive(g2, g2_number)
    arrive(w2, w_number)

    rows = Z * YL * tokens

    def partial(k, carry):
        mine = g[:, c].reshape(rows, g.shape[-1])
        theirs = g2[...].reshape(rows, g.shape[-1])
        at = pl.ds(pl.multiple_of(k * chunk, chunk), chunk)
        dims = (((1,), (1,)), ((), ()))
        total = (lax.dot_general(mine, w[at, :], dims, preferred_element_type=F32)
                 + lax.dot_general(theirs, w2[at, :], dims, preferred_element_type=F32))
        pf[:, k] = total.reshape(Z * YL, tokens, chunk)
        return carry

    sum_lo, sum_hi = pl.ds(0, sum_chunks), pl.ds(sum_chunks, T - sum_chunks)
    sum_halves = {"lo": sum_lo, "hi": sum_hi}
    sums = {(sign, piece, s): pair() for sign in (1, -1) for piece in pieces for s in range(4)}
    back_numbers = {}

    def target(rel, zz):
        return block(rel, zz, 0) // C

    def give_across(away):
        i = away + 4
        ybs[i] = pf[target(1, z + ahead * away), sum_hi].astype(BF16)
        back_numbers[away] = pair()
        send(ybs.at[i], ybr.at[i], yp, back_numbers[away])

    def reduce_piece(s, piece):
        rel, half, far = piece
        part = sum_halves[half]
        for sign in (1, -1):
            if s == 0 and sign != far:
                continue
            into, out_of, to = (rp, sbp, zp) if sign == 1 else (rm, sbm, zm)
            away = sign * (4 - s)
            total = pf[target(rel, z + ahead * away), part]
            if half == "hi":
                arrive(ybr.at[away + 4], back_numbers[away])
                total = total + ybr[away + 4].astype(F32)
            if s > 1 or (s == 1 and sign == far):
                arrive(into.at[rel, s - 1, part], sums[sign, piece, s - 1])
                total = total + into[rel, s - 1, part].astype(F32)
            out_of[rel, s, part] = total.astype(BF16)
            send(out_of.at[rel, s, part], into.at[rel, s, part], to, sums[sign, piece, s])

    order = (pieces[1], pieces[2], pieces[0])

    def reduce_step(s):
        for piece in order:
            reduce_piece(s, piece)

    lax.fori_loop(0, sum_chunks, partial, 0)
    reduce_piece(0, order[0])
    reduce_piece(0, order[1])
    ring_step(2)
    lax.fori_loop(sum_chunks, T, partial, 0)
    across_step(0)
    for away in (4, 3, -3, 2, -2, 1, -1, 0):
        give_across(away)
    across_step(1)
    ring_step(3)
    reduce_piece(0, order[2])
    reduce_step(1)
    across_step(2)

    def products(i, carry):
        total = jnp.zeros((256, w.shape[1]), F32)
        for k in range(T):
            lhs = r[pl.ds(8 * i, 8), k].reshape(256, chunk)
            total = total + jnp.dot(lhs, w[k * chunk:(k + 1) * chunk, :], preferred_element_type=F32)
        q[i // 2, pl.ds(2 * (i % 2), 2)] = total.reshape(2, 128, w.shape[1]).astype(BF16)
        return carry

    def weight_grad(k, carry):
        lhs = r[:, k].reshape(2 * rows, chunk)
        rhs = g[...].reshape(2 * rows, g.shape[-1])
        total = lax.dot_general(lhs, rhs, (((0,), (0,)), ((), ())), preferred_element_type=F32)
        at = pl.ds(pl.multiple_of(k * chunk, chunk), chunk)
        wg[at, :] = total * grad_scale
        return carry

    across_step(3)
    for b, part, number in to_sib:
        arrive(r.at[b, part], number)
    lax.fori_loop(0, 2, products, 0)
    reduce_step(2)
    lax.fori_loop(2, 4, products, 0)
    out_numbers = [pair() for _ in along_x]
    for j, peer in enumerate(along_x):
        send(q.at[:, (x + j + 1) % X], xq.at[x], peer, out_numbers[j])
    xq[x] = q[:, x]
    reduce_step(3)
    lax.fori_loop(0, 3, weight_grad, 0)

    def finals(piece):
        rel, half, far = piece
        part = sum_halves[half]
        total = pf[target(rel, z), part]
        for sign, into in ((1, rp), (-1, rm)):
            arrive(into.at[rel, 3, part], sums[sign, piece, 3])
            total = total + into[rel, 3, part].astype(F32)
        return total

    ys[...] = finals(order[0]).astype(BF16)
    back_number = pair()
    send(ys, yr, yp, back_number)
    rg[sum_lo] = finals(order[1])
    arrive(ybr.at[4], back_numbers[0])
    rg[sum_hi] = finals(order[2]) + ybr[4].astype(F32)
    lax.fori_loop(3, 5, weight_grad, 0)
    arrive(yr, back_number)
    rg[sum_lo] = rg[sum_lo] + yr[...].astype(F32)
    for k, part in enumerate(local_rotation([rg[k] for k in range(T)])):
        t1[k] = part.astype(BF16)
    first_done = rotate_first(t1, v1)

    def out_sum(half):
        total = xq[0, half].astype(F32)
        for k in range(1, X):
            total = total + xq[k, half].astype(F32)
        return total

    for j in range(1, X):
        arrive(xq.at[(x + X - j) % X], out_numbers[j - 1])
    os[...] = out_sum(1 - yh).astype(BF16)
    last_number = pair()
    send(os, oa, opposite, last_number)
    first_done()
    finish = rotate_second(v1, t2, igb)
    lax.fori_loop(5, 8, weight_grad, 0)
    total = out_sum(yh)
    arrive(oa, last_number)
    out[...] = (total + oa[...].astype(F32)).astype(BF16)

    finish()
    for k in range(T):
        ing[:, k * chunk:(k + 1) * chunk] = igb[k]

    for copy in sent:
        copy.wait_send()

    assert used[0] <= SEMS, used[0]


def place(out_in, ing_in, wg_in, out, ing, wg, sems):
    rows = wg.shape[0] // T
    copies = [pltpu.make_async_copy(out_in, out, sems.at[T]),
              pltpu.make_async_copy(ing_in, ing, sems.at[T + 1])]
    for i in range(T):
        at = pl.ds(i * rows, rows)
        copies.append(pltpu.make_async_copy(wg_in.at[at], wg.at[at], sems.at[i]))
    for copy in copies:
        copy.start()
    for copy in copies:
        copy.wait()


def per_device(activations, weight, out_grad):
    tokens, width = activations.shape
    features = weight.shape[1]
    groups = YL * Z * C
    chunk = width // T
    scale = 1.0 / math.sqrt(width * T)
    grad_scale = 1.0 / math.sqrt(tokens * groups)
    had = jnp.asarray(signs_table(chunk), BF16)
    vmem = pl.BlockSpec(memory_space=pltpu.VMEM)
    anywhere = pl.BlockSpec(memory_space=pl.ANY)
    part = (T, tokens, chunk)
    low = (SUM_CHUNKS, tokens, chunk)
    high = (T - SUM_CHUNKS, tokens, chunk)
    shapes = (
        jax.ShapeDtypeStruct((out_grad.shape[0], features), BF16),
        jax.ShapeDtypeStruct((tokens, width), BF16),
        jax.ShapeDtypeStruct((width, features), F32),
    )
    results = pl.pallas_call(
        functools.partial(kernel, scale, grad_scale, LO_CHUNKS, SUM_CHUNKS),
        out_shape=tuple(pltpu.VMEM(leaf.shape, leaf.dtype) for leaf in shapes),
        in_specs=[pl.BlockSpec(memory_space=pltpu.HBM)] * 4,
        out_specs=(vmem,) * 3,
        scratch_shapes=[
            pltpu.VMEM((tokens, width), BF16),
            pltpu.VMEM((width, features), BF16),
            pltpu.VMEM((2, C, tokens, features), BF16),
            pltpu.VMEM((chunk, chunk), BF16),
            pltpu.VMEM((width, features), BF16),
            pltpu.VMEM(part, F32), pltpu.VMEM(part, F32), pltpu.VMEM(part, BF16),
            pltpu.VMEM((groups,) + part, BF16),
            pltpu.VMEM((groups // C, C, tokens, features), BF16),
            pltpu.VMEM((groups // C, tokens, features), BF16),
            pltpu.VMEM((groups // C,) + part, F32),
            pltpu.VMEM((2, 4) + part, BF16), pltpu.VMEM((2, 4) + part, BF16),
            pltpu.VMEM((2, 4) + part, BF16), pltpu.VMEM((2, 4) + part, BF16),
            pltpu.VMEM((9,) + high, BF16), pltpu.VMEM((9,) + high, BF16),
            pltpu.VMEM(low, BF16), pltpu.VMEM(low, BF16),
            pltpu.VMEM((T // X, X, out_grad.shape[0], features), BF16),
            pltpu.VMEM((X, T // X, out_grad.shape[0], features), BF16),
            pltpu.VMEM((out_grad.shape[0], features), BF16),
            pltpu.VMEM((out_grad.shape[0], features), BF16),
            pltpu.VMEM(part, BF16), pltpu.VMEM(part, BF16),
            pltpu.VMEM(part, BF16), pltpu.VMEM(part, BF16),
                pltpu.VMEM(part, F32),
            pltpu.SemaphoreType.DMA((SEMS,)),
            pltpu.SemaphoreType.DMA((T + 4,)),
        ],
        compiler_params=pltpu.CompilerParams(
            collective_id=0, has_side_effects=True, vmem_limit_bytes=237 << 18),
        name="rotated_projection",
    )(activations, weight, out_grad.reshape(2, C, tokens, features), had)
    return pl.pallas_call(
        place,
        out_shape=shapes,
        in_specs=[vmem] * 3,
        out_specs=(anywhere,) * 3,
        scratch_shapes=[pltpu.SemaphoreType.DMA((T + 2,))],
        compiler_params=pltpu.CompilerParams(vmem_limit_bytes=16 << 20),
        name="place_results",
    )(*results)


def solution(mesh):
    return jax.shard_map(
        per_device,
        mesh=mesh,
        in_specs=(P("dp", "tensor"), P("tensor", "dp"), P("tensor", "dp")),
        out_specs=(P("tensor", "dp"), P("dp", "tensor"), P("tensor", "dp")),
        check_vma=False,
    )
```

```python
import functools
import math

import jax
import jax.numpy as jnp
import numpy as np
from jax import lax
from jax.experimental import pallas as pl
from jax.experimental.pallas import tpu as pltpu
from jax.sharding import PartitionSpec as P

MESH = pl.DeviceIdType.MESH
YL, Z, C, T, X = 2, 8, 2, 8, 4
LO_CHUNKS = 4
SUM_CHUNKS = 7
F32, BF16 = jnp.float32, jnp.bfloat16
SEMS = 320


def signs_table(width):
    position = np.arange(width)
    joined = position[:, None] & position[None, :]
    parity = np.zeros_like(joined)
    for bit_number in range(width.bit_length() - 1):
        parity = parity + ((joined >> bit_number) & 1)
    return np.where(parity % 2 == 1, -1.0, 1.0)


def butterfly(parts):
    parts = list(parts)
    apart = 1
    while apart < len(parts):
        for low in range(len(parts)):
            if low & apart == 0:
                a, b = parts[low], parts[low | apart]
                parts[low], parts[low | apart] = a + b, a - b
        apart *= 2
    return parts


def kernel(scale, grad_scale, lo_chunks, sum_chunks, act_hbm, w_hbm, og_hbm, had_hbm, out, ing, wg, act, w, og, had,
           w2, s1, x1, s2, r, g, g2, pf, sbp, sbm, rp, rm, ybs, ybr, ys, yr, q, xq, os, oa, t1, v1, t2, igb,
           rg, sems, local_sems):
    d, t = lax.axis_index("dp"), lax.axis_index("tensor")
    c, z, yl = d % C, (d // C) % Z, d // (C * Z)
    yh, x = t // X, t % X
    ahead = 1 - 2 * c
    tokens, width = act.shape
    chunk = width // T
    lo, hi = pl.ds(0, lo_chunks), pl.ds(lo_chunks, T - lo_chunks)

    def block(rel, zz, core):
        return (((yl + rel) % YL) * Z + (zz + 2 * Z) % Z) * C + core

    sib = (block(0, z, 1 - c), t)
    zp, zm = (block(0, z + ahead, c), t), (block(0, z - ahead, c), t)
    yp = (block(1, z, c), t)
    peers = [(d, (t + j) % T) for j in range(1, T)]
    opposite = (d, (t + X) % T)
    along_x = [(d, yh * X + (x + j) % X) for j in range(1, X)]

    barrier = pltpu.get_barrier_semaphore()
    everyone = [sib, zp, zm, yp] + peers
    for other in everyone:
        pl.semaphore_signal(barrier, inc=1, device_id=other, device_id_type=MESH)
    loads = [pltpu.make_async_copy(src, dst, local_sems.at[T + i])
             for i, (src, dst) in enumerate(((act_hbm, act), (had_hbm, had), (og_hbm, og), (w_hbm, w)))]
    for load in loads:
        load.start()
    loads[0].wait()
    loads[1].wait()

    used = [0]
    sent = []

    def pair():
        used[0] += 2
        return used[0] - 2

    def remote(src, dst, to, number):
        return pltpu.make_async_remote_copy(
            src_ref=src, dst_ref=dst, send_sem=sems.at[number], recv_sem=sems.at[number + 1],
            device_id=to, device_id_type=MESH)

    def send(src, dst, to, number):
        copy = remote(src, dst, to, number)
        copy.start()
        sent.append(copy)

    def arrive(dst, number):
        remote(dst, dst, sib, number).wait_recv()

    def local_rotation(parts):
        rows = jnp.concatenate(parts, axis=0)
        table = had[...]
        if rows.dtype == BF16:
            mixed = jnp.dot(rows, table, preferred_element_type=F32)
        else:
            high = rows.astype(BF16)
            rest = rows - high.astype(F32)
            middle = rest.astype(BF16)
            low = (rest - middle.astype(F32)).astype(BF16)
            mixed = (jnp.dot(high, table, preferred_element_type=F32)
                     + jnp.dot(middle, table, preferred_element_type=F32)
                     + jnp.dot(low, table, preferred_element_type=F32))
        return butterfly([mixed[k * tokens:(k + 1) * tokens] for k in range(T)])

    def rotate_first(first, first_in):
        numbers = [pair() for _ in peers]
        for j, peer in enumerate(peers):
            send(first.at[peer[1]], first_in.at[t], peer, numbers[j])
        first_in[t] = first[t]

        def finish():
            for j in range(1, T):
                arrive(first_in.at[(t + T - j) % T], numbers[j - 1])

        return finish

    def rotate_second(first_in, second, landing):
        for k, part in enumerate(butterfly([first_in[k].astype(F32) for k in range(T)])):
            second[k] = (part * scale).astype(BF16)
        numbers = [pair() for _ in peers]
        for j, peer in enumerate(peers):
            send(second.at[peer[1]], landing.at[t], peer, numbers[j])
        landing[t] = second[t]

        def finish():
            for j in range(1, T):
                arrive(landing.at[(t + T - j) % T], numbers[j - 1])

        return finish

    own = block(0, z, c)
    for k, part in enumerate(local_rotation([act[:, k * chunk:(k + 1) * chunk] for k in range(T)])):
        s1[k] = part
    pl.semaphore_wait(barrier, len(everyone))
    first_done = rotate_first(s1, x1)
    loads[2].wait()

    def grad_rows(tt):
        return g.at[pl.ds(2 * tt, 2)]

    opposite_number = pair()
    send(og, grad_rows(t), opposite, opposite_number)
    g[pl.ds(2 * t, 2)] = og[...]
    loads[3].wait()
    w_number = pair()
    send(w, w2, sib, w_number)
    first_done()
    finish = rotate_second(x1, s2, r.at[own])
    near_numbers = [pair() for _ in along_x]
    for j, peer in enumerate(along_x):
        send(og, grad_rows(t), peer, near_numbers[j])
    opposite_t = (t + X) % T
    arrive(grad_rows(opposite_t), opposite_number)
    far_numbers = [pair() for _ in along_x]
    for j, peer in enumerate(along_x):
        send(grad_rows(opposite_t), grad_rows(opposite_t), peer, far_numbers[j])
    finish()

    to_sib = []

    def share(rel, zz, part):
        number = pair()
        send(r.at[block(rel, zz, c), part], r.at[block(rel, zz, c), part], sib, number)
        to_sib.append((block(rel, zz, 1 - c), part, number))

    pieces = ((0, "hi", 1), (1, "lo", 1), (0, "lo", -1))
    halves = {"lo": lo, "hi": hi}
    numbers = {(sign, piece, s): pair() for sign in (1, -1) for piece in pieces for s in range(4)}
    across_numbers = {}

    def pass_on(sign, piece, zz, s):
        view = r.at[block(piece[0], zz, c), halves[piece[1]]]
        send(view, view, zp if sign == 1 else zm, numbers[sign, piece, s])

    def across(zz, step):
        across_numbers[step] = pair()
        view = r.at[block(0, zz, c), hi]
        send(view, view, yp, across_numbers[step])

    def across_arrive(zz, step):
        arrive(r.at[block(1, zz, c), hi], across_numbers[step])
        share(1, zz, hi)

    y_number = pair()
    send(r.at[own, lo], r.at[own, lo], yp, y_number)
    for piece in pieces:
        if piece[0] == 0:
            pass_on(1, piece, z, 0)
            pass_on(-1, piece, z, 0)
    share(0, z, lo)
    share(0, z, hi)
    arrive(r.at[block(1, z, c), lo], y_number)
    pass_on(1, pieces[1], z, 0)
    pass_on(-1, pieces[1], z, 0)
    across(z, 0)
    share(1, z, lo)

    def ring_piece(s, piece):
        rel, half, far = piece
        for sign in (1, -1):
            if s == 3 and sign != far:
                continue
            zz = z - sign * ahead * (1 + s)
            arrive(r.at[block(rel, zz, c), halves[half]], numbers[sign, piece, s])
            if s < 2 or (s == 2 and sign == far):
                pass_on(sign, piece, zz, s + 1)
            if rel == 0 and half == "hi":
                across(zz, sign * (1 + s))
            share(rel, zz, halves[half])

    def ring_step(s):
        for piece in pieces:
            ring_piece(s, piece)

    def across_step(s):
        for sign in (1, -1):
            if s < 3 or sign == 1:
                across_arrive(z - sign * ahead * (1 + s), sign * (1 + s))

    ring_step(0)
    for j in range(1, X):
        from_x = (x + X - j) % X
        arrive(grad_rows(yh * X + from_x), near_numbers[j - 1])
        arrive(grad_rows((1 - yh) * X + from_x), far_numbers[j - 1])
    g2_number = pair()
    send(g.at[:, 1 - c], g2, sib, g2_number)
    across_arrive(z, 0)
    ring_step(1)
    arrive(g2, g2_number)
    arrive(w2, w_number)

    rows = Z * YL * tokens

    def partial(k, carry):
        mine = g[:, c].reshape(rows, g.shape[-1])
        theirs = g2[...].reshape(rows, g.shape[-1])
        at = pl.ds(pl.multiple_of(k * chunk, chunk), chunk)
        dims = (((1,), (1,)), ((), ()))
        total = (lax.dot_general(mine, w[at, :], dims, preferred_element_type=F32)
                 + lax.dot_general(theirs, w2[at, :], dims, preferred_element_type=F32))
        pf[:, k] = total.reshape(Z * YL, tokens, chunk)
        return carry

    sum_lo, sum_hi = pl.ds(0, sum_chunks), pl.ds(sum_chunks, T - sum_chunks)
    sum_halves = {"lo": sum_lo, "hi": sum_hi}
    sums = {(sign, piece, s): pair() for sign in (1, -1) for piece in pieces for s in range(4)}
    back_numbers = {}

    def target(rel, zz):
        return block(rel, zz, 0) // C

    def give_across(away):
        i = away + 4
        ybs[i] = pf[target(1, z + ahead * away), sum_hi].astype(BF16)
        back_numbers[away] = pair()
        send(ybs.at[i], ybr.at[i], yp, back_numbers[away])

    def reduce_piece(s, piece):
        rel, half, far = piece
        part = sum_halves[half]
        for sign in (1, -1):
            if s == 0 and sign != far:
                continue
            into, out_of, to = (rp, sbp, zp) if sign == 1 else (rm, sbm, zm)
            away = sign * (4 - s)
            total = pf[target(rel, z + ahead * away), part]
            if half == "hi":
                arrive(ybr.at[away + 4], back_numbers[away])
                total = total + ybr[away + 4].astype(F32)
            if s > 1 or (s == 1 and sign == far):
                arrive(into.at[rel, s - 1, part], sums[sign, piece, s - 1])
                total = total + into[rel, s - 1, part].astype(F32)
            out_of[rel, s, part] = total.astype(BF16)
            send(out_of.at[rel, s, part], into.at[rel, s, part], to, sums[sign, piece, s])

    order = (pieces[1], pieces[2], pieces[0])

    def reduce_step(s):
        for piece in order:
            reduce_piece(s, piece)

    lax.fori_loop(0, sum_chunks, partial, 0)
    reduce_piece(0, order[0])
    reduce_piece(0, order[1])
    ring_step(2)
    lax.fori_loop(sum_chunks, T, partial, 0)
    across_step(0)
    for away in (4, 3, -3, 2, -2, 1, -1, 0):
        give_across(away)
    across_step(1)
    ring_step(3)
    reduce_piece(0, order[2])
    reduce_step(1)
    across_step(2)

    def products(i, carry):
        total = jnp.zeros((256, w.shape[1]), F32)
        for k in range(T):
            lhs = r[pl.ds(8 * i, 8), k].reshape(256, chunk)
            total = total + jnp.dot(lhs, w[k * chunk:(k + 1) * chunk, :], preferred_element_type=F32)
        q[i // 2, pl.ds(2 * (i % 2), 2)] = total.reshape(2, 128, w.shape[1]).astype(BF16)
        return carry

    def weight_grad(k, carry):
        lhs = r[:, k].reshape(2 * rows, chunk)
        rhs = g[...].reshape(2 * rows, g.shape[-1])
        total = lax.dot_general(lhs, rhs, (((0,), (0,)), ((), ())), preferred_element_type=F32)
        at = pl.ds(pl.multiple_of(k * chunk, chunk), chunk)
        wg[at, :] = total * grad_scale
        return carry

    across_step(3)
    for b, part, number in to_sib:
        arrive(r.at[b, part], number)
    lax.fori_loop(0, 2, products, 0)
    reduce_step(2)
    lax.fori_loop(2, 4, products, 0)
    out_numbers = [pair() for _ in along_x]
    for j, peer in enumerate(along_x):
        send(q.at[:, (x + j + 1) % X], xq.at[x], peer, out_numbers[j])
    xq[x] = q[:, x]
    reduce_step(3)
    lax.fori_loop(0, 3, weight_grad, 0)

    def finals(piece):
        rel, half, far = piece
        part = sum_halves[half]
        total = pf[target(rel, z), part]
        for sign, into in ((1, rp), (-1, rm)):
            arrive(into.at[rel, 3, part], sums[sign, piece, 3])
            total = total + into[rel, 3, part].astype(F32)
        return total

    ys[...] = finals(order[0]).astype(BF16)
    back_number = pair()
    send(ys, yr, yp, back_number)
    rg[sum_lo] = finals(order[1])
    arrive(ybr.at[4], back_numbers[0])
    rg[sum_hi] = finals(order[2]) + ybr[4].astype(F32)
    lax.fori_loop(3, 5, weight_grad, 0)
    arrive(yr, back_number)
    rg[sum_lo] = rg[sum_lo] + yr[...].astype(F32)
    for k, part in enumerate(local_rotation([rg[k] for k in range(T)])):
        t1[k] = part.astype(BF16)
    first_done = rotate_first(t1, v1)

    def out_sum(half):
        total = xq[0, half].astype(F32)
        for k in range(1, X):
            total = total + xq[k, half].astype(F32)
        return total

    for j in range(1, X):
        arrive(xq.at[(x + X - j) % X], out_numbers[j - 1])
    os[...] = out_sum(1 - yh).astype(BF16)
    last_number = pair()
    send(os, oa, opposite, last_number)
    first_done()
    finish = rotate_second(v1, t2, igb)
    lax.fori_loop(5, 8, weight_grad, 0)
    total = out_sum(yh)
    arrive(oa, last_number)
    out[...] = (total + oa[...].astype(F32)).astype(BF16)

    finish()
    for k in range(T):
        ing[:, k * chunk:(k + 1) * chunk] = igb[k]

    for copy in sent:
        copy.wait_send()

    assert used[0] <= SEMS, used[0]


def place(out_in, ing_in, wg_in, out, ing, wg, sems):
    rows = wg.shape[0] // T
    copies = [pltpu.make_async_copy(out_in, out, sems.at[T]),
              pltpu.make_async_copy(ing_in, ing, sems.at[T + 1])]
    for i in range(T):
        at = pl.ds(i * rows, rows)
        copies.append(pltpu.make_async_copy(wg_in.at[at], wg.at[at], sems.at[i]))
    for copy in copies:
        copy.start()
    for copy in copies:
        copy.wait()


def per_device(activations, weight, out_grad):
    tokens, width = activations.shape
    features = weight.shape[1]
    groups = YL * Z * C
    chunk = width // T
    scale = 1.0 / math.sqrt(width * T)
    grad_scale = 1.0 / math.sqrt(tokens * groups)
    had = jnp.asarray(signs_table(chunk), BF16)
    vmem = pl.BlockSpec(memory_space=pltpu.VMEM)
    anywhere = pl.BlockSpec(memory_space=pl.ANY)
    part = (T, tokens, chunk)
    low = (SUM_CHUNKS, tokens, chunk)
    high = (T - SUM_CHUNKS, tokens, chunk)
    shapes = (
        jax.ShapeDtypeStruct((out_grad.shape[0], features), BF16),
        jax.ShapeDtypeStruct((tokens, width), BF16),
        jax.ShapeDtypeStruct((width, features), F32),
    )
    results = pl.pallas_call(
        functools.partial(kernel, scale, grad_scale, LO_CHUNKS, SUM_CHUNKS),
        out_shape=tuple(pltpu.VMEM(leaf.shape, leaf.dtype) for leaf in shapes),
        in_specs=[pl.BlockSpec(memory_space=pltpu.HBM)] * 4,
        out_specs=(vmem,) * 3,
        scratch_shapes=[
            pltpu.VMEM((tokens, width), BF16),
            pltpu.VMEM((width, features), BF16),
            pltpu.VMEM((2, C, tokens, features), BF16),
            pltpu.VMEM((chunk, chunk), BF16),
            pltpu.VMEM((width, features), BF16),
            pltpu.VMEM(part, F32), pltpu.VMEM(part, F32), pltpu.VMEM(part, BF16),
            pltpu.VMEM((groups,) + part, BF16),
            pltpu.VMEM((groups // C, C, tokens, features), BF16),
            pltpu.VMEM((groups // C, tokens, features), BF16),
            pltpu.VMEM((groups // C,) + part, F32),
            pltpu.VMEM((2, 4) + part, BF16), pltpu.VMEM((2, 4) + part, BF16),
            pltpu.VMEM((2, 4) + part, BF16), pltpu.VMEM((2, 4) + part, BF16),
            pltpu.VMEM((9,) + high, BF16), pltpu.VMEM((9,) + high, BF16),
            pltpu.VMEM(low, BF16), pltpu.VMEM(low, BF16),
            pltpu.VMEM((T // X, X, out_grad.shape[0], features), BF16),
            pltpu.VMEM((X, T // X, out_grad.shape[0], features), BF16),
            pltpu.VMEM((out_grad.shape[0], features), BF16),
            pltpu.VMEM((out_grad.shape[0], features), BF16),
            pltpu.VMEM(part, BF16), pltpu.VMEM(part, BF16),
            pltpu.VMEM(part, BF16), pltpu.VMEM(part, BF16),
                pltpu.VMEM(part, F32),
            pltpu.SemaphoreType.DMA((SEMS,)),
            pltpu.SemaphoreType.DMA((T + 4,)),
        ],
        compiler_params=pltpu.CompilerParams(
            collective_id=0, has_side_effects=True, vmem_limit_bytes=237 << 18),
        name="rotated_projection",
    )(activations, weight, out_grad.reshape(2, C, tokens, features), had)
    return pl.pallas_call(
        place,
        out_shape=shapes,
        in_specs=[vmem] * 3,
        out_specs=(anywhere,) * 3,
        scratch_shapes=[pltpu.SemaphoreType.DMA((T + 2,))],
        compiler_params=pltpu.CompilerParams(vmem_limit_bytes=16 << 20),
        name="place_results",
    )(*results)


def solution(mesh):
    return jax.shard_map(
        per_device,
        mesh=mesh,
        in_specs=(P("dp", "tensor"), P("tensor", "dp"), P("tensor", "dp")),
        out_specs=(P("tensor", "dp"), P("dp", "tensor"), P("tensor", "dp")),
        check_vma=False,
    )
```
